32 devices in a mesh: face: 4 (over x, core), sub: 8 (over z, y).
Axes of the slice: x: 2, y: 2, z: 4, core: 2. Of those that a mesh axis runs over, the one named last changes fastest.
Arguments:
- grid_inputs: bfloat16 [131072, 474], P(('face', 'sub')), may hold values from -6 to 6
- mesh_nodes: bfloat16 [10240, 512], P(('face', 'sub')), may hold values from -6 to 6
- encoder_edges: bfloat16 [4, 256, 512], P(None, ('face', 'sub')), may hold values from -6 to 6
- mesh_edges: bfloat16 [4, 81920], P(None, ('face', 'sub')), may hold values from -6 to 6
- grid_send: int32 [256, 512], P(('face', 'sub')), may hold values from -1 to 4095, as said below
- node_receive: int32 [256, 512], P(('face', 'sub')), may hold values from -1 to 319, as said below
- halo_send: int32 [1024, 16], P(('face', 'sub')), may hold values from -1 to 319, as said below
- edge_source: int32 [81920], P(('face', 'sub')), may hold values from 0 to 831, as said below
- edge_target: int32 [81920], P(('face', 'sub')), may hold values from 0 to 319
- embed_first: bfloat16 [474, 512], replicated, may hold values from -0.09186304 to 0.09186304
- embed_second: bfloat16 [512, 512], replicated, may hold values from -0.088388348 to 0.088388348
- encoder_feature: bfloat16 [4, 512], replicated, may hold values from -1.75 to 1.75
- encoder_sender: bfloat16 [512, 512], replicated, may hold values from -0.05103104 to 0.05103104
- encoder_receiver: bfloat16 [512, 512], replicated, may hold values from -0.15625 to 0.15625
- encoder_output: bfloat16 [512, 512], replicated, may hold values from -0.25 to 0.25
- updater_self: bfloat16 [512, 512], replicated, may hold values from -0.1875 to 0.1875
- updater_message: bfloat16 [512, 512], replicated, may hold values from -0.1875 to 0.1875
- updater_output: bfloat16 [512, 512], replicated, may hold values from -0.25 to 0.25
- processor_feature: bfloat16 [4, 512], replicated, may hold values from -1.75 to 1.75
- processor_sender: bfloat16 [512, 512], replicated, may hold values from -0.05103104 to 0.05103104
- processor_receiver: bfloat16 [512, 512], replicated, may hold values from -0.15625 to 0.15625
- processor_output: bfloat16 [512, 512], replicated, may hold values from -0.25 to 0.25
- refiner_self: bfloat16 [512, 512], replicated, may hold values from -0.1875 to 0.1875
- refiner_message: bfloat16 [512, 512], replicated, may hold values from -0.1875 to 0.1875
- refiner_output: bfloat16 [512, 512], replicated, may hold values from -0.25 to 0.25
Outputs:
- mesh_state: bfloat16 [10240, 512], P(('face', 'sub'))
The draws below stay inside these ranges and needn't reach their ends.
Inputs may be any that keep to these rules, and one draw needn't show every extreme that they name: `grid_send`: on tile (f, s), row r lists up to 512 slots of grid-to-mesh edges toward tile (f, r); the used slots of a row come first, -1 marks an empty slot. In every face group one tile receives full rows from all 8 sources. `node_receive`: on tile (f, r), entry [s, k] is the receiving local mesh node of the edge in slot k of row r of grid_send on tile (f, s); -1 exactly where that slot is empty. `halo_send`: on tile p, row q lists up to 16 local mesh nodes that tile q reads; used slots come first, -1 marks an empty slot, row p is empty. One tile receives full rows from every other tile. `edge_source`: index into the receiving tile's table of its 320 nodes followed by the 32 x 16 slots sent to it, source-major (slot k from tile p at 320 + p * 16 + k). Every used slot sent to a tile is read by exactly one of its edges; no empty slot is read.
All inputs are finite; a program needn't handle non-finite values.
Results may differ from the reference program's by a relative error of at most 0.0095.
Values may be sent and summed in bfloat16 or wider, within the bound.
A program may use at most 128 MiB of HBM per device.

```python
import math
import jax
import jax.numpy as jnp
from jax import lax

D = 512
INCH = 474
EFEAT = 4
GRID_DEV = 4096
MESH_DEV = 320
CAP = 512
HCAP = 16
MEDGE_DEV = 2560
FACES = 4
SUBS = 8
DEVS = 32
GRID = 131072
MESH = 10240
MEDGE = 81920


def grid_tables(key):
    base = jax.random.fold_in(key, 101)
    count_key, fullest_key, grid_key, node_key = jax.random.split(base, 4)
    counts = jax.random.randint(count_key, (FACES, SUBS, SUBS), 0, CAP + 1)
    fullest = jax.random.randint(fullest_key, (FACES,), 0, SUBS)
    target = jnp.arange(SUBS)[None, None, :]
    counts = jnp.where(target == fullest[:, None, None], CAP, counts)
    lacking = (fullest + 1) % SUBS
    counts = jnp.where(target == lacking[:, None, None], jnp.minimum(counts, CAP - 1), counts)
    slot_index = jnp.arange(CAP)[None, None, None, :]
    occupied = slot_index < counts[..., None]
    grid_rows = jax.random.randint(grid_key, (FACES, SUBS, SUBS, CAP), 0, GRID_DEV)
    node_rows = jax.random.randint(node_key, (FACES, SUBS, SUBS, CAP), 0, MESH_DEV)
    forced = (target[..., None] == fullest[:, None, None, None]) & (slot_index == 0)
    grid_rows = jnp.where(forced, GRID_DEV - 1, grid_rows)
    node_rows = jnp.where(forced, MESH_DEV - 1, node_rows)
    return (occupied, grid_rows, node_rows)


def draw_grid_send(key, part):
    occupied, grid_rows, node_rows = grid_tables(key)
    return jnp.where(occupied, grid_rows, -1).reshape(FACES * SUBS * SUBS, CAP).astype(jnp.int32)


def draw_node_receive(key, part):
    occupied, grid_rows, node_rows = grid_tables(key)
    received = jnp.where(occupied, node_rows, -1).transpose(0, 2, 1, 3)
    return received.reshape(FACES * SUBS * SUBS, CAP).astype(jnp.int32)


def halo_tables(key):
    base = jax.random.fold_in(key, 202)
    count_key, fullest_key, node_key, local_key, target_key, shuffle_key = jax.random.split(base, 6)
    counts = jax.random.randint(count_key, (DEVS, DEVS), 0, HCAP + 1)
    fullest = jax.random.randint(fullest_key, (), 0, DEVS - 1)
    source = jnp.arange(DEVS)[:, None]
    target = jnp.arange(DEVS)[None, :]
    counts = jnp.where(target == fullest, HCAP, counts)
    counts = jnp.where(source == target, 0, counts)
    slot_index = jnp.arange(HCAP)[None, None, :]
    occupied = slot_index < counts[..., None]
    node_rows = jax.random.randint(node_key, (DEVS, DEVS, HCAP), 0, MESH_DEV)
    forced = (source[..., None] == DEVS - 1) & (target[..., None] == fullest) & (slot_index == 0)
    node_rows = jnp.where(forced, MESH_DEV - 1, node_rows)
    halo = jnp.where(occupied, node_rows, -1)
    arriving = occupied.transpose(1, 0, 2).reshape(DEVS, DEVS * HCAP)
    ordering = jnp.argsort(jnp.where(arriving, 0, 1).astype(jnp.int32), axis=1, stable=True).astype(jnp.int32)
    ordering = jnp.pad(ordering, ((0, 0), (0, MEDGE_DEV - DEVS * HCAP)))
    live_count = jnp.sum(arriving.astype(jnp.int32), axis=1)
    edge_index = jnp.arange(MEDGE_DEV)[None, :]
    local_slot = jax.random.randint(local_key, (DEVS, MEDGE_DEV), 0, MESH_DEV)
    local_slot = jnp.where(edge_index == live_count[:, None], 0, local_slot)
    source_slot = jnp.where(edge_index < live_count[:, None], MESH_DEV + ordering, local_slot)
    scores = jax.random.randint(shuffle_key, (DEVS, MEDGE_DEV), 0, MEDGE_DEV) * MEDGE_DEV + edge_index
    shuffle = jnp.argsort(scores, axis=1)
    source_slot = jnp.take_along_axis(source_slot, shuffle, axis=1)
    targets = jax.random.randint(target_key, (DEVS, MEDGE_DEV), 0, MESH_DEV)
    targets = jnp.where(edge_index == 0, MESH_DEV - 1, targets)
    targets = jnp.where(edge_index == 1, 0, targets)
    return (halo, source_slot, targets)


def draw_halo_send(key, part):
    halo, source_slot, targets = halo_tables(key)
    return halo.reshape(DEVS * DEVS, HCAP).astype(jnp.int32)


def draw_edge_source(key, part):
    halo, source_slot, targets = halo_tables(key)
    return source_slot.reshape(DEVS * MEDGE_DEV).astype(jnp.int32)


def draw_edge_target(key, part):
    halo, source_slot, targets = halo_tables(key)
    return targets.reshape(DEVS * MEDGE_DEV).astype(jnp.int32)


def cosine_weight(key, row_count, column_count, fan_in):
    row_key, column_key, row_sign_key, column_sign_key, noise_key = jax.random.split(key, 5)
    frequency = jax.random.permutation(row_key, column_count)[:row_count].astype(jnp.int32)
    position = jax.random.permutation(column_key, column_count).astype(jnp.int32)
    phase = (2 * position[None, :] + 1) * frequency[:, None] % (4 * column_count)
    table = jnp.cos(jnp.pi * phase.astype(jnp.float32) / (2.0 * column_count)) * math.sqrt(2.0 / column_count)
    table = jnp.where(frequency[:, None] == 0, math.sqrt(1.0 / column_count), table)
    row_sign = (jax.random.randint(row_sign_key, (row_count,), 0, 2) * 2 - 1).astype(jnp.float32)
    column_sign = (jax.random.randint(column_sign_key, (column_count,), 0, 2) * 2 - 1).astype(jnp.float32)
    noise = jnp.clip(jax.random.normal(noise_key, (row_count, column_count), jnp.float32), -4.0, 4.0)
    noise = noise * (0.1 / math.sqrt(column_count))
    values = row_sign[:, None] * column_sign[None, :] * table + noise
    return (values * math.sqrt(column_count / fan_in)).astype(jnp.float32)


def draw_embed_first(key, part):
    return cosine_weight(jax.random.fold_in(key, 301), INCH, D, INCH).astype(jnp.bfloat16)


def draw_embed_second(key, part):
    return cosine_weight(jax.random.fold_in(key, 302), D, D, D).astype(jnp.bfloat16)


def draw_encoder_sender(key, part):
    return cosine_weight(jax.random.fold_in(key, 303), D, D, 3 * D).astype(jnp.bfloat16)


def draw_processor_sender(key, part):
    return cosine_weight(jax.random.fold_in(key, 304), D, D, 3 * D).astype(jnp.bfloat16)


def block_levels(rng, extent, pieces, smallest, top_value):
    loudness, own = 1.0, jax.random.fold_in(rng, 6)
    for dim, shards_of in pieces:
        heights = jnp.exp(jax.random.uniform(jax.random.fold_in(own, dim), (shards_of,), jnp.float32, smallest / len(pieces), top_value / len(pieces)))
        loudness = loudness * jnp.repeat(heights, extent[dim] // shards_of).reshape([-1 if axis == dim else 1 for axis in range(len(extent))])
    return loudness


def normal_values(stream_key, dims, width, limit, shards=(), kind=jnp.bfloat16):
    drawn = jax.random.normal(stream_key, dims, jnp.float32) * width
    if len(shards) > 0:
        drawn = block_levels(stream_key, dims, shards, -0.22, 0.18) * drawn
    return jnp.clip(drawn, min=-limit, max=limit).astype(kind)


def setup_inputs(seed: int = 0) -> dict:
    streams_of = jax.random.split(jax.random.key(seed), 26)
    return {
        "grid_inputs": normal_values(streams_of[0], (GRID, INCH), 1.0, 6.0, ((0, 32),)),
        "mesh_nodes": normal_values(streams_of[1], (MESH, D), 1.0, 6.0, ((0, 32),)),
        "encoder_edges": normal_values(streams_of[2], (EFEAT, DEVS * SUBS, CAP), 1.0, 6.0, ((1, 32),)),
        "mesh_edges": normal_values(streams_of[3], (EFEAT, MEDGE), 1.0, 6.0, ((1, 32),)),
        "grid_send": draw_grid_send(jax.random.fold_in(streams_of[25], 71), 0),
        "node_receive": draw_node_receive(jax.random.fold_in(streams_of[25], 71), 0),
        "halo_send": draw_halo_send(jax.random.fold_in(streams_of[25], 71), 0),
        "edge_source": draw_edge_source(jax.random.fold_in(streams_of[25], 71), 0),
        "edge_target": draw_edge_target(jax.random.fold_in(streams_of[25], 71), 0),
        "embed_first": draw_embed_first(jax.random.fold_in(streams_of[25], 71), 0),
        "embed_second": draw_embed_second(jax.random.fold_in(streams_of[25], 71), 0),
        "encoder_feature": normal_values(streams_of[11], (EFEAT, D), (3 * EFEAT) ** -0.5, 1.75),
        "encoder_sender": draw_encoder_sender(jax.random.fold_in(streams_of[25], 71), 0),
        "encoder_receiver": normal_values(streams_of[13], (D, D), (3 * D) ** -0.5, 0.15625),
        "encoder_output": normal_values(streams_of[14], (D, D), D ** -0.5, 0.25),
        "updater_self": normal_values(streams_of[15], (D, D), (2 * D) ** -0.5, 0.1875),
        "updater_message": normal_values(streams_of[16], (D, D), (2 * D) ** -0.5, 0.1875),
        "updater_output": normal_values(streams_of[17], (D, D), D ** -0.5, 0.25),
        "processor_feature": normal_values(streams_of[18], (EFEAT, D), (3 * EFEAT) ** -0.5, 1.75),
        "processor_sender": draw_processor_sender(jax.random.fold_in(streams_of[25], 71), 0),
        "processor_receiver": normal_values(streams_of[20], (D, D), (3 * D) ** -0.5, 0.15625),
        "processor_output": normal_values(streams_of[21], (D, D), D ** -0.5, 0.25),
        "refiner_self": normal_values(streams_of[22], (D, D), (2 * D) ** -0.5, 0.1875),
        "refiner_message": normal_values(streams_of[23], (D, D), (2 * D) ** -0.5, 0.1875),
        "refiner_output": normal_values(streams_of[24], (D, D), D ** -0.5, 0.25),
    }


EPSILON = 1e-05

def layer_norm(values):
    row_mean = lax.optimization_barrier(jnp.mean(values, axis=-1, keepdims=True))
    centered = values - row_mean
    spread = lax.optimization_barrier(jnp.mean(centered * centered, axis=-1, keepdims=True))
    return centered * lax.rsqrt(spread + EPSILON)

def embed_rows(inputs, first_weight, second_weight):
    hidden = jax.nn.silu(jnp.dot(inputs, first_weight, preferred_element_type=jnp.float32)).astype(jnp.bfloat16)
    return layer_norm(jnp.dot(hidden, second_weight, preferred_element_type=jnp.float32)).astype(jnp.bfloat16)

def edge_message(summed, output_weight):
    hidden = jax.nn.silu(summed).astype(jnp.bfloat16)
    return layer_norm(jnp.dot(hidden, output_weight, preferred_element_type=jnp.float32)).astype(jnp.bfloat16)

def node_update(node_state, aggregate, self_weight, message_weight, output_weight):
    summed = jnp.dot(node_state, self_weight, preferred_element_type=jnp.float32)
    summed = summed + jnp.dot(aggregate.astype(jnp.bfloat16), message_weight, preferred_element_type=jnp.float32)
    hidden = jax.nn.silu(summed).astype(jnp.bfloat16)
    refined = layer_norm(jnp.dot(hidden, output_weight, preferred_element_type=jnp.float32))
    return (node_state.astype(jnp.float32) + refined).astype(jnp.bfloat16)

def reference(grid_inputs, mesh_nodes, encoder_edges, mesh_edges, grid_send, node_receive, halo_send, edge_source, edge_target, embed_first, embed_second, encoder_feature, encoder_sender, encoder_receiver, encoder_output, updater_self, updater_message, updater_output, processor_feature, processor_sender, processor_receiver, processor_output, refiner_self, refiner_message, refiner_output):
    feature_count = encoder_edges.shape[0]
    face_grid = grid_inputs.reshape(FACES, SUBS * GRID_DEV, INCH)
    face_send = grid_send.reshape(FACES, SUBS, SUBS, CAP)
    face_receive = node_receive.reshape(FACES, SUBS, SUBS, CAP)
    face_edges = encoder_edges.reshape(feature_count, FACES, SUBS, SUBS, CAP).transpose(1, 2, 3, 4, 0)
    face_nodes = mesh_nodes.reshape(FACES, SUBS * MESH_DEV, D)
    tile_index = jnp.arange(SUBS).astype(jnp.int32)

    def encode_face(operands):
        grid_rows, send_rows, receive_rows, edge_rows, node_state = operands
        latent = embed_rows(grid_rows, embed_first, embed_second)
        sender_term = jnp.dot(latent, encoder_sender, preferred_element_type=jnp.float32)
        receiver_term = jnp.dot(node_state, encoder_receiver, preferred_element_type=jnp.float32)
        send_aligned = send_rows.transpose(1, 0, 2)
        occupied = (send_aligned >= 0).reshape(-1)
        grid_index = (tile_index[None, :, None] * GRID_DEV + jnp.maximum(send_aligned, 0).astype(jnp.int32)).reshape(-1)
        node_index = (tile_index[:, None, None] * MESH_DEV + jnp.maximum(receive_rows, 0).astype(jnp.int32)).reshape(-1)
        summed = jnp.dot(edge_rows.reshape(-1, feature_count), encoder_feature, preferred_element_type=jnp.float32)
        summed = summed + sender_term[grid_index] + receiver_term[node_index]
        message = edge_message(summed, encoder_output).astype(jnp.float32)
        message = jnp.where(occupied[:, None], message, jnp.zeros_like(message))
        aggregate = jax.ops.segment_sum(message, node_index, num_segments=SUBS * MESH_DEV)
        return node_update(node_state, aggregate, updater_self, updater_message, updater_output)
    state = lax.map(encode_face, (face_grid, face_send, face_receive, face_edges, face_nodes)).reshape(MESH, D)
    device_index = jnp.arange(DEVS).astype(jnp.int32)
    halo_grid = jnp.maximum(halo_send, 0).astype(jnp.int32).reshape(DEVS, DEVS, HCAP)
    remote_global = (device_index[:, None, None] * MESH_DEV + halo_grid).transpose(1, 0, 2).reshape(DEVS, DEVS * HCAP)
    local_global = device_index[:, None] * MESH_DEV + jnp.arange(MESH_DEV).astype(jnp.int32)[None, :]
    table_global = jnp.concatenate([local_global.astype(jnp.int32), remote_global.astype(jnp.int32)], axis=1)
    source_global = jnp.take_along_axis(table_global, edge_source.reshape(DEVS, MEDGE_DEV).astype(jnp.int32), axis=1)
    sender_all = jnp.dot(state, processor_sender, preferred_element_type=jnp.float32)
    device_edges = mesh_edges.reshape(feature_count, DEVS, MEDGE_DEV).transpose(1, 2, 0)

    def process_device(operands):
        sources, targets, edge_rows, node_state = operands
        receiver_term = jnp.dot(node_state, processor_receiver, preferred_element_type=jnp.float32)
        summed = jnp.dot(edge_rows, processor_feature, preferred_element_type=jnp.float32)
        summed = summed + sender_all[sources] + receiver_term[targets]
        message = edge_message(summed, processor_output).astype(jnp.float32)
        aggregate = jax.ops.segment_sum(message, targets, num_segments=MESH_DEV)
        return node_update(node_state, aggregate, refiner_self, refiner_message, refiner_output)
    result = lax.map(process_device, (source_global, edge_target.reshape(DEVS, MEDGE_DEV).astype(jnp.int32), device_edges, state.reshape(DEVS, MESH_DEV, D)))
    return result.reshape(MESH, D)
```

```python
import functools

import jax
import jax.numpy as jnp
from jax import lax
from jax.experimental import pallas as pl
from jax.experimental.pallas import tpu as pltpu
from jax.sharding import PartitionSpec as P

EPSILON = 1e-05
LANES = 128
MESH_ID = pl.DeviceIdType.MESH


def silu(values):
    half = values * 0.5
    return (half + half * jnp.tanh(half)).astype(jnp.bfloat16)


def norm(values):
    width = values.shape[-1]
    centered = values - jnp.sum(values, axis=-1, keepdims=True) * (1.0 / width)
    spread = jnp.sum(centered * centered, axis=-1, keepdims=True) * (1.0 / width)
    return centered * lax.rsqrt(spread + EPSILON)


def dot(a, b):
    return jnp.dot(a, b, preferred_element_type=jnp.float32)


def dot_t(a, b):
    return lax.dot_general(a, b, (((0,), (0,)), ((), ())), preferred_element_type=jnp.float32)


def pick(count, index):
    rows = lax.broadcasted_iota(jnp.int32, (count, index.shape[1]), 0)
    return jnp.where(rows == index, 1.0, 0.0).astype(jnp.bfloat16)


def sub_at(position, subs):
    position = lax.rem(position + subs, subs)
    return jnp.where(position < subs // 2, 2 * position, 2 * (subs - 1 - position) + 1)


def ring_position(subs):
    sub = lax.axis_index("sub")
    return jnp.where(lax.rem(sub, 2) == 0, sub // 2, subs - 1 - sub // 2)


def ring_order(subs):
    order = []
    for distance in range(1, subs // 2):
        order += [subs - distance, distance]
    return order + [subs // 2, 0]


def device_at(position, subs):
    return (lax.axis_index("face"), sub_at(position, subs))


def embed_kernel(
    chunk,
    subs,
    index_ref,
    x_ref,
    first_ref,
    second_ref,
    sender_ref,
    nodes_ref,
    aux_ref,
    out_ref,
    nodes_out,
    aux_out,
    table,
    slots,
    slot_sem,
    own_sem,
    ring_send,
    ring_recv,
    aux_send,
    aux_recv,
):
    step = pl.program_id(0)
    steps = pl.num_programs(0)
    rows, width = x_ref.shape[1], second_ref.shape[1]
    nodes, half = nodes_ref.shape[0], nodes_ref.shape[0] // 2
    parts = width // LANES
    capacity = index_ref.shape[1]
    order = ring_order(subs)
    place_of = {distance: place for place, distance in enumerate(order)}
    here = ring_position(subs)

    def ring(flow, hop):
        sign = 1 - 2 * flow
        span = pl.ds(flow * half, half)
        old = place_of[(-sign * hop) % subs]
        new = place_of[(-sign * (hop + 1)) % subs]
        return pltpu.make_async_remote_copy(
            src_ref=nodes_ref.at[span, :] if hop == 0 else nodes_out.at[old, span, :],
            dst_ref=nodes_out.at[new, span, :],
            send_sem=ring_send.at[flow, hop],
            recv_sem=ring_recv.at[flow, hop],
            device_id=device_at(here + sign, subs),
            device_id_type=MESH_ID,
        )

    def side(distance):
        return pltpu.make_async_remote_copy(
            src_ref=aux_ref.at[sub_at(here + distance, subs)],
            dst_ref=aux_out.at[place_of[subs - distance]],
            send_sem=aux_send.at[distance],
            recv_sem=aux_recv.at[distance],
            device_id=device_at(here + distance, subs),
            device_id_type=MESH_ID,
        )

    def own():
        place = place_of[0]
        return (
            pltpu.make_async_copy(nodes_ref, nodes_out.at[place], own_sem.at[0]),
            pltpu.make_async_copy(aux_ref.at[sub_at(here, subs)], aux_out.at[place], own_sem.at[1]),
        )

    def forward(hop):
        for flow in range(2):
            ring(flow, hop - 1).wait_recv()
            ring(flow, hop).start()

    @pl.when(step == 0)
    def _():
        barrier = pltpu.get_barrier_semaphore()
        for distance in range(1, subs):
            pl.semaphore_signal(
                barrier, inc=1, device_id=device_at(here + distance, subs), device_id_type=MESH_ID
            )
        pl.semaphore_wait(barrier, subs - 1)
        for flow in range(2):
            ring(flow, 0).start()
        for distance in range(1, subs):
            side(distance).start()
        for copy in own():
            copy.start()

    hidden = silu(dot_t(x_ref[...], first_ref[...]))
    latent = norm(dot(hidden, second_ref[...])).astype(jnp.bfloat16)
    sent = dot(latent, sender_ref[...])
    base = pl.multiple_of(step * rows, rows)
    for part in range(parts):
        table[pl.ds(base, rows), part, :] = sent[:, part * LANES : (part + 1) * LANES]

    @pl.when(step == steps // 2 - 1)
    def _():
        forward(1)

    @pl.when(step == steps - 1)
    def _():
        forward(2)
        done = 2

        def move(place):
            return pltpu.make_async_copy(slots.at[place], out_ref.at[place], slot_sem.at[place])

        for place, distance in enumerate(order):
            target = sub_at(here + distance, subs)

            @pl.loop(0, capacity // chunk)
            def _(block):
                for slot in range(chunk):
                    spot = block * chunk + slot
                    slots[place, spot] = table[index_ref[target, spot]]

            move(place).start()
            while done < 2 + ((place + 1) * (subs - 4)) // subs:
                done += 1
                forward(done)
        for flow in range(2):
            ring(flow, subs - 2).wait_recv()
            for hop in range(subs - 1):
                ring(flow, hop).wait_send()
        for distance in range(1, subs):
            side(distance).wait()
        for copy in own():
            copy.wait()
        for place in range(subs):
            move(place).wait()


def edge_kernel(
    block,
    subs,
    sent_ref,
    nodes_ref,
    aux_ref,
    receiver_ref,
    feature_ref,
    output_ref,
    out_ref,
    acc,
    table,
    kept,
    outbox,
    inbox,
    ring_send,
    ring_recv,
):
    step = pl.program_id(0)
    nodes, width = nodes_ref.shape[1], nodes_ref.shape[2]
    half = nodes // 2
    capacity = aux_ref.shape[2]
    parts = width // LANES
    order = ring_order(subs)
    here = ring_position(subs)

    @pl.when(step == 0)
    def _():
        barrier = pltpu.get_barrier_semaphore()
        for distance in (1, subs - 1):
            pl.semaphore_signal(
                barrier, inc=1, device_id=device_at(here + distance, subs), device_id_type=MESH_ID
            )

    table[:nodes, :] = dot(nodes_ref[0], receiver_ref[...]).astype(jnp.bfloat16)
    table[nodes:, :] = feature_ref[...]
    aux = aux_ref[0]
    values = aux[:8, :].astype(jnp.float32)
    index = (values[4:5, :] * 16.0 + values[5:6, :]).astype(jnp.int32)
    for start in range(0, capacity, block):
        chosen = pick(nodes, index[:, start : start + block])
        wide = jnp.concatenate([chosen, aux[:, start : start + block]], axis=0)
        sent = jnp.concatenate(
            [
                sent_ref[0, start : start + block, part, :]
                for part in range(parts)
            ],
            axis=1,
        )
        summed = dot_t(wide, table[...]) + sent
        message = norm(dot(silu(summed), output_ref[...])).astype(jnp.bfloat16)
        if start == 0:
            acc[...] = dot(chosen, message)
        else:
            acc[...] += dot(chosen, message)
    kept[step] = acc[...].astype(jnp.bfloat16)

    def ring(flow, hop):
        sign = 1 - 2 * flow
        return pltpu.make_async_remote_copy(
            src_ref=outbox.at[flow, hop],
            dst_ref=inbox.at[flow, hop],
            send_sem=ring_send.at[flow, hop],
            recv_sem=ring_recv.at[flow, hop],
            device_id=device_at(here + sign, subs),
            device_id_type=MESH_ID,
        )

    def push(flow, hop):
        sign = 1 - 2 * flow
        place = order.index((-sign * (hop + 1)) % subs)
        own = kept[place, flow * half : (flow + 1) * half, :]
        if hop == 0:
            outbox[flow, hop] = own
        else:
            ring(flow, hop - 1).wait_recv()
            total = own.astype(jnp.float32) + inbox[flow, hop - 1].astype(jnp.float32)
            outbox[flow, hop] = total.astype(jnp.bfloat16)
        ring(flow, hop).start()

    for place in range(subs):
        distance = order[place]

        @pl.when(step == place)
        def _():
            if place == 0:
                pl.semaphore_wait(pltpu.get_barrier_semaphore(), 2)
            if distance == 0:
                for hop in range(subs // 2, subs - 1):
                    for flow in range(2):
                        push(flow, hop)
                for flow in range(2):
                    ring(flow, subs - 2).wait_recv()
                    span = slice(flow * half, (flow + 1) * half)
                    total = acc[span, :] + inbox[flow, subs - 2].astype(jnp.float32)
                    out_ref[span, :] = total.astype(jnp.bfloat16)
                for flow in range(2):
                    for hop in range(subs - 1):
                        ring(flow, hop).wait_send()
            elif distance == subs // 2:
                for flow in range(2):
                    push(flow, distance - 1)
            elif distance > subs // 2:
                push(0, subs - distance - 1)
            else:
                push(1, distance - 1)


def partner(step, faces, subs):
    face, sub = lax.axis_index("face"), lax.axis_index("sub")
    return flip(face, lax.rem(step, faces), faces), flip(sub, step // faces, subs)


def flip(index, mask, count):
    total, bit = 0, 1
    while bit < count:
        total = total + lax.rem(lax.rem(index // bit, 2) + lax.rem(mask // bit, 2), 2) * bit
        bit *= 2
    return total


def processor_kernel(
    block,
    faces,
    subs,
    nodes_ref,
    sum_ref,
    halo_ref,
    source_ref,
    target_ref,
    edges_ref,
    feature_ref,
    *rest,
):
    weights, rest = rest[:9], rest[9:]
    (
        out_ref,
        held,
        held_sem,
        outgoing,
        arrived,
        local_table,
        base,
        acc,
        send_sem,
        recv_sem,
    ) = rest

    def fetch(place):
        return pltpu.make_async_copy(weights[place], held.at[place], held_sem.at[place])

    for place in range(len(weights)):
        fetch(place).start()

    def weight(place):
        fetch(place).wait()
        return held[place]

    devices = faces * subs
    me = lax.axis_index("face") * subs + lax.axis_index("sub")
    nodes, width = nodes_ref.shape
    slots = halo_ref.shape[1] // devices
    table_slots = devices * slots
    edges = source_ref.shape[1]
    barrier = pltpu.get_barrier_semaphore()

    @pl.loop(1, devices)
    def _(step):
        face, sub = partner(step, faces, subs)
        pl.semaphore_signal(barrier, inc=1, device_id=(face, sub), device_id_type=MESH_ID)

    start = nodes_ref[...]
    before = dot(start, weight(0)) + dot(sum_ref[...], weight(1))
    refined = norm(dot(silu(before), weight(2)))
    state = (start.astype(jnp.float32) + refined).astype(jnp.bfloat16)
    outgoing[...] = dot_t(pick(nodes, halo_ref[...]), state).astype(jnp.bfloat16)
    arrived[pl.ds(pl.multiple_of(me * slots, slots), slots), :] = jnp.zeros(
        (slots, width), jnp.bfloat16
    )
    pl.semaphore_wait(barrier, devices - 1)

    def copy(step):
        face, sub = partner(step, faces, subs)
        other = face * subs + sub
        return pltpu.make_async_remote_copy(
            src_ref=outgoing.at[pl.ds(pl.multiple_of(other * slots, slots), slots), :],
            dst_ref=arrived.at[pl.ds(pl.multiple_of(me * slots, slots), slots), :],
            send_sem=send_sem.at[step],
            recv_sem=recv_sem.at[step],
            device_id=(face, sub),
            device_id_type=MESH_ID,
        )

    @pl.loop(1, devices)
    def _(step):
        copy(devices - step).start()

    local_table[:nodes, :] = dot(state, weight(3)).astype(jnp.bfloat16)
    local_table[nodes : 2 * nodes, :] = dot(state, weight(4)).astype(jnp.bfloat16)
    local_table[2 * nodes :, :] = feature_ref[...]
    own_part = dot(state, weight(6))

    group = min(512, table_slots)
    source = source_ref[...]
    target = target_ref[...]
    tags = edges_ref[...]
    high = (target // 16).astype(jnp.float32)
    low = (target - (target // 16) * 16).astype(jnp.float32)
    digits = jnp.concatenate(
        [high, low, jnp.ones_like(high), jnp.zeros((13, edges), jnp.float32)], axis=0
    ).astype(jnp.bfloat16)
    info = jnp.concatenate([tags, digits], axis=0)
    spots = []
    for first in range(0, table_slots, group):
        rows = lax.broadcasted_iota(jnp.int32, (group, edges), 0) + (nodes + first)
        reads = jnp.where(rows == source, 1.0, 0.0).astype(jnp.bfloat16)
        found = lax.dot_general(
            reads, info, (((1,), (1,)), ((), ())), preferred_element_type=jnp.float32
        )
        spot = found[:, 16:17] * 16.0 + found[:, 17:18] + found[:, 18:19] - 1.0
        spot = spot.astype(jnp.int32)
        lanes = lax.broadcasted_iota(jnp.int32, (group, nodes), 1)
        chosen = jnp.where(lanes == spot, 1.0, 0.0).astype(jnp.bfloat16)
        base[first : first + group, :] = dot(chosen, local_table[nodes : 2 * nodes, :]) + dot(
            found[:, :16].astype(jnp.bfloat16), local_table[2 * nodes :, :]
        )
        spots.append(chosen)

    fetch(5).wait()
    for first in range(0, edges, block):
        span = slice(first, first + block)
        wide = jnp.concatenate(
            [
                pick(nodes, source_ref[:, span]),
                pick(nodes, target_ref[:, span]),
                edges_ref[:, span],
            ],
            axis=0,
        )
        total = dot_t(wide, local_table[...])
        message = norm(dot(silu(total), held[5])).astype(jnp.bfloat16)
        kept = jnp.where(source_ref[:, span] < nodes, target_ref[:, span], -1)
        if first == 0:
            acc[...] = dot(pick(nodes, kept), message)
        else:
            acc[...] += dot(pick(nodes, kept), message)

    @pl.loop(1, devices)
    def _(step):
        copy(devices - step).wait()

    for place, first in enumerate(range(0, table_slots, group)):
        span = slice(first, first + group)
        total = base[span, :] + dot(arrived[span, :], held[3])
        message = norm(dot(silu(total), held[5])).astype(jnp.bfloat16)
        acc[...] += dot_t(spots[place], message)
    after = own_part + dot(acc[...].astype(jnp.bfloat16), weight(7))
    final = norm(dot(silu(after), weight(8)))
    out_ref[...] = (state.astype(jnp.float32) + final).astype(jnp.bfloat16)


def vmem():
    return pl.BlockSpec(memory_space=pltpu.VMEM)


def smem():
    return pl.BlockSpec(memory_space=pltpu.SMEM)


def shards(
    grid_inputs,
    mesh_nodes,
    encoder_edges,
    mesh_edges,
    grid_send,
    node_receive,
    halo_send,
    edge_source,
    edge_target,
    embed_first,
    embed_second,
    encoder_feature,
    encoder_sender,
    encoder_receiver,
    encoder_output,
    updater_self,
    updater_message,
    updater_output,
    processor_feature,
    processor_sender,
    processor_receiver,
    processor_output,
    refiner_self,
    refiner_message,
    refiner_output,
):
    subs = lax.axis_size("sub")
    faces = lax.axis_size("face")
    devices = subs * faces
    grid_rows, inputs = grid_inputs.shape
    nodes, width = mesh_nodes.shape
    capacity = grid_send.shape[1]
    parts = width // LANES
    feats = encoder_edges.shape[0]

    receive = jnp.stack([node_receive >> 4, node_receive & 15]).astype(jnp.bfloat16)
    aux = jnp.concatenate(
        [encoder_edges, receive, jnp.zeros((16 - feats - 2, subs, capacity), jnp.bfloat16)], axis=0
    ).transpose(1, 0, 2)
    rows = 512
    whole = lambda shape: pl.BlockSpec(shape, lambda i: (0,) * len(shape))
    anywhere = pl.BlockSpec(memory_space=pl.ANY)
    sent, face_nodes, face_aux = pl.pallas_call(
        functools.partial(embed_kernel, min(64, capacity), subs),
        grid=(grid_rows // rows,),
        out_shape=(
            jax.ShapeDtypeStruct((subs, capacity, parts, LANES), jnp.float32),
            jax.ShapeDtypeStruct((subs, nodes, width), jnp.bfloat16),
            jax.ShapeDtypeStruct((subs, 16, capacity), jnp.bfloat16),
        ),
        in_specs=[
            smem(),
            pl.BlockSpec((inputs, rows), lambda i: (0, i)),
            whole((inputs, width)),
            whole((width, width)),
            whole((width, width)),
            vmem(),
            vmem(),
        ],
        out_specs=(anywhere, anywhere, anywhere),
        scratch_shapes=[
            pltpu.VMEM((grid_rows, parts, LANES), jnp.float32),
            pltpu.VMEM((subs, capacity, parts, LANES), jnp.float32),
            pltpu.SemaphoreType.DMA((subs,)),
            pltpu.SemaphoreType.DMA((2,)),
            pltpu.SemaphoreType.DMA((2, subs - 1)),
            pltpu.SemaphoreType.DMA((2, subs - 1)),
            pltpu.SemaphoreType.DMA((subs,)),
            pltpu.SemaphoreType.DMA((subs,)),
        ],
        compiler_params=pltpu.CompilerParams(
            collective_id=1, has_side_effects=True, vmem_limit_bytes=56 * 2**20
        ),
        name="embed",
    )(
        jnp.maximum(grid_send, 0),
        grid_inputs.T,
        embed_first,
        embed_second,
        encoder_sender,
        mesh_nodes,
        aux,
    )

    pad_feature = lambda weight: jnp.pad(weight, ((0, 16 - feats), (0, 0)))
    mine = lambda shape: pl.BlockSpec((1,) + shape, lambda i: (i, 0, 0))
    half = nodes // 2
    summed = pl.pallas_call(
        functools.partial(edge_kernel, min(256, capacity), subs),
        grid=(subs,),
        in_specs=[
            pl.BlockSpec((1, capacity, parts, LANES), lambda i: (i, 0, 0, 0)),
            mine((nodes, width)),
            mine((16, capacity)),
            whole((width, width)),
            whole((16, width)),
            whole((width, width)),
        ],
        out_specs=whole((nodes, width)),
        scratch_shapes=[
            pltpu.VMEM((nodes, width), jnp.float32),
            pltpu.VMEM((nodes + 16, width), jnp.bfloat16),
            pltpu.VMEM((subs, nodes, width), jnp.bfloat16),
            pltpu.VMEM((2, subs - 1, half, width), jnp.bfloat16),
            pltpu.VMEM((2, subs - 1, half, width), jnp.bfloat16),
            pltpu.SemaphoreType.DMA((2, subs - 1)),
            pltpu.SemaphoreType.DMA((2, subs - 1)),
        ],
        out_shape=jax.ShapeDtypeStruct((nodes, width), jnp.bfloat16),
        compiler_params=pltpu.CompilerParams(
            collective_id=2, has_side_effects=True, vmem_limit_bytes=60 * 2**20
        ),
        name="edges",
    )(sent, face_nodes, face_aux, encoder_receiver, pad_feature(encoder_feature), encoder_output)

    edge_count = edge_source.shape[0]
    halo = halo_send.reshape(1, -1)
    step = min(512, edge_count)
    operands = (
        mesh_nodes,
        summed,
        halo,
        edge_source.reshape(1, -1),
        edge_target.reshape(1, -1),
        jnp.pad(mesh_edges, ((0, 16 - feats), (0, 0))),
        pad_feature(processor_feature),
        updater_self,
        updater_message,
        updater_output,
        processor_sender,
        processor_receiver,
        processor_output,
        refiner_self,
        refiner_message,
        refiner_output,
    )
    return pl.pallas_call(
        functools.partial(processor_kernel, step, faces, subs),
        out_shape=jax.ShapeDtypeStruct((nodes, width), jnp.bfloat16),
        in_specs=[vmem()] * (len(operands) - 9) + [anywhere] * 9,
        out_specs=vmem(),
        scratch_shapes=[
            pltpu.VMEM((9, width, width), jnp.bfloat16),
            pltpu.SemaphoreType.DMA((9,)),
            pltpu.VMEM((halo.shape[1], width), jnp.bfloat16),
            pltpu.VMEM((halo.shape[1], width), jnp.bfloat16),
            pltpu.VMEM((2 * nodes + 16, width), jnp.bfloat16),
            pltpu.VMEM((halo.shape[1], width), jnp.float32),
            pltpu.VMEM((nodes, width), jnp.float32),
            pltpu.SemaphoreType.DMA((devices,)),
            pltpu.SemaphoreType.DMA((devices,)),
        ],
        compiler_params=pltpu.CompilerParams(
            collective_id=0, has_side_effects=True, vmem_limit_bytes=60 * 2**20
        ),
        name="processor",
    )(*operands)


def solution(mesh):
    rows = P(("face", "sub"), None)
    placed = (
        rows,
        rows,
        P(None, ("face", "sub"), None),
        P(None, ("face", "sub")),
        rows,
        rows,
        rows,
        P(("face", "sub")),
        P(("face", "sub")),
    ) + (P(),) * 16
    return jax.shard_map(
        shards, mesh=mesh, in_specs=placed, out_specs=P(("face", "sub"), None), check_vma=False
    )
```

```python
import functools

import jax
import jax.numpy as jnp
from jax import lax
from jax.experimental import pallas as pl
from jax.experimental.pallas import tpu as pltpu
from jax.sharding import PartitionSpec as P

EPSILON = 1e-05
LANES = 128
MESH_ID = pl.DeviceIdType.MESH


def silu(values):
    half = values * 0.5
    return (half + half * jnp.tanh(half)).astype(jnp.bfloat16)


def norm(values):
    width = values.shape[-1]
    centered = values - jnp.sum(values, axis=-1, keepdims=True) * (1.0 / width)
    spread = jnp.sum(centered * centered, axis=-1, keepdims=True) * (1.0 / width)
    return centered * lax.rsqrt(spread + EPSILON)


def dot(a, b):
    return jnp.dot(a, b, preferred_element_type=jnp.float32)


def dot_t(a, b):
    return lax.dot_general(a, b, (((0,), (0,)), ((), ())), preferred_element_type=jnp.float32)


def pick(count, index):
    rows = lax.broadcasted_iota(jnp.int32, (count, index.shape[1]), 0)
    return jnp.where(rows == index, 1.0, 0.0).astype(jnp.bfloat16)


def sub_at(position, subs):
    position = lax.rem(position + subs, subs)
    return jnp.where(position < subs // 2, 2 * position, 2 * (subs - 1 - position) + 1)


def ring_position(subs):
    sub = lax.axis_index("sub")
    return jnp.where(lax.rem(sub, 2) == 0, sub // 2, subs - 1 - sub // 2)


def device_at(position, subs):
    return (lax.axis_index("face"), sub_at(position, subs))


def ring_distance(place, subs):
    half = lax.div(place + 1, 2)
    ahead = subs // 2 - half
    return jnp.where(lax.rem(place, 2) == 1, ahead, lax.rem(subs // 2 + half, subs))


def encoder_kernel(
    rows,
    subs,
    index_ref,
    edges_ref,
    receive_ref,
    feature_ref,
    x_hbm,
    nodes_hbm,
    first_hbm,
    second_hbm,
    sender_hbm,
    receiver_hbm,
    output_hbm,
    out_ref,
    x,
    nodes,
    first,
    square,
    load_sem,
    x_sem,
    table,
    picked,
    aux,
    aux_in,
    terms,
    wide_table,
    acc,
    kept,
    outbox,
    inbox,
    side_send,
    side_recv,
    gather_send,
    gather_recv,
    sum_send,
    sum_recv,
):
    count, width = nodes.shape
    feats = edges_ref.shape[0]
    capacity = index_ref.shape[1]
    points = x.shape[1]
    parts = width // LANES
    far = subs // 2
    pieces = 4
    piece = count // pieces
    steps = points // rows
    here = ring_position(subs)

    loads = [
        pltpu.make_async_copy(nodes_hbm, nodes, load_sem.at[0]),
        pltpu.make_async_copy(receiver_hbm, square.at[0], load_sem.at[1]),
        pltpu.make_async_copy(first_hbm, first, load_sem.at[2]),
        pltpu.make_async_copy(second_hbm, square.at[1], load_sem.at[3]),
        pltpu.make_async_copy(sender_hbm, square.at[2], load_sem.at[4]),
        pltpu.make_async_copy(output_hbm, square.at[3], load_sem.at[5]),
    ]

    def load_x(step):
        span = pl.ds(pl.multiple_of(step * rows, rows), rows)
        return pltpu.make_async_copy(x_hbm.at[:, span], x.at[:, span], x_sem.at[step])

    loads[0].start()
    loads[1].start()
    loads[2].start()
    load_x(0).start()
    loads[3].start()
    loads[4].start()

    @pl.loop(1, steps)
    def _(step):
        load_x(step).start()

    loads[5].start()

    barrier = pltpu.get_barrier_semaphore()
    for distance in range(1, subs):
        pl.semaphore_signal(
            barrier, inc=1, device_id=device_at(here + distance, subs), device_id_type=MESH_ID
        )

    received = receive_ref[...]
    high = lax.div(received + 16, 16) - 1
    low = (received - high * 16).astype(jnp.float32)
    high = high.astype(jnp.float32)
    tags = [edges_ref[feat].astype(jnp.float32) for feat in range(feats)]
    fill = jnp.zeros((8 - feats - 2, capacity), jnp.float32)
    for source in range(subs):
        span = slice(source, source + 1)
        block = jnp.concatenate(
            [tag[span, :] for tag in tags] + [high[span, :], low[span, :], fill], axis=0
        )
        aux[source] = jnp.concatenate(
            [block[:, : capacity // 2], block[:, capacity // 2 :]], axis=0
        ).astype(jnp.bfloat16)
    table[0] = jnp.zeros((parts, LANES), jnp.float32)
    wide_table[count:, :] = jnp.zeros((16, width), jnp.bfloat16)
    wide_table[count : count + feats, :] = feature_ref[...]

    loads[0].wait()
    loads[1].wait()
    terms[0] = dot(nodes[...], square[0]).astype(jnp.bfloat16)
    pl.semaphore_wait(barrier, subs - 1)

    def gather(flow, hop, part):
        sign = 1 - 2 * flow
        span = pl.ds((2 * flow + part) * piece, piece)
        return pltpu.make_async_remote_copy(
            src_ref=terms.at[(-sign * hop) % subs, span, :],
            dst_ref=terms.at[(-sign * (hop + 1)) % subs, span, :],
            send_sem=gather_send.at[flow, 2 * hop + part],
            recv_sem=gather_recv.at[flow, 2 * hop + part],
            device_id=device_at(here + sign, subs),
            device_id_type=MESH_ID,
        )

    relays = 2 * (subs - 2)

    def relay(event):
        hop, part = event // 2 + 1, event % 2
        for flow in range(2):
            gather(flow, hop - 1, part).wait_recv()
            gather(flow, hop, part).start()

    def side(distance):
        return pltpu.make_async_remote_copy(
            src_ref=aux.at[sub_at(here + distance, subs)],
            dst_ref=aux_in.at[subs - distance],
            send_sem=side_send.at[distance],
            recv_sem=side_recv.at[distance],
            device_id=device_at(here + distance, subs),
            device_id_type=MESH_ID,
        )

    for part in range(2):
        for flow in range(2):
            gather(flow, 0, part).start()
    for distance in range(1, subs):
        side(distance).start()
    aux_in[0] = aux[sub_at(here, subs)]

    for load in loads[2:5]:
        load.wait()

    done = min(steps - 1, relays)

    @pl.loop(0, steps)
    def _(step):
        load_x(step).wait()
        start = pl.multiple_of(step * rows, rows)
        hidden = silu(dot_t(x[:, pl.ds(start, rows)], first[...]))
        latent = norm(dot(hidden, square[1])).astype(jnp.bfloat16)
        sent = dot(latent, square[2])
        for part in range(parts):
            table[pl.ds(start + 1, rows), part, :] = sent[:, part * LANES : (part + 1) * LANES]
        for event in range(done):

            @pl.when(step == event + 1)
            def _():
                relay(event)

    loads[5].wait()

    def pass_on(flow, stage, part):
        sign = 1 - 2 * flow
        span = pl.ds(part * piece, piece)
        return pltpu.make_async_remote_copy(
            src_ref=outbox.at[flow, stage - 1, span, :],
            dst_ref=inbox.at[flow, stage - 1, span, :],
            send_sem=sum_send.at[flow, stage - 1, part],
            recv_sem=sum_recv.at[flow, stage - 1, part],
            device_id=device_at(here + sign, subs),
            device_id_type=MESH_ID,
        )

    def has(flow, stage, part):
        return stage < far or part // 2 == flow

    def place_of(flow, stage):
        if stage == far:
            return 0
        return 2 * (far - stage) - 1 + flow

    def push(flow, stage, part):
        span = slice(part * piece, (part + 1) * piece)
        value = kept[place_of(flow, stage), span, :]
        if stage < far and has(flow, stage + 1, part):
            pass_on(flow, stage + 1, part).wait_recv()
            value = value.astype(jnp.float32) + inbox[flow, stage, span, :].astype(jnp.float32)
            value = value.astype(jnp.bfloat16)
        outbox[flow, stage - 1, span, :] = value
        pass_on(flow, stage, part).start()

    def push_early(stage):
        for part in range(2):
            for flow in range(2):
                if stage == far:
                    push(flow, stage, 2 * flow + part)
                else:
                    push(flow, stage, 2 * (1 - flow) + part)

    def push_late(stage):
        for part in range(2):
            for flow in range(2):
                push(flow, stage, 2 * flow + part)

    events = {place: [] for place in range(subs)}
    events[0].append(functools.partial(push_early, far))
    for turn in range(1, far):
        early = min(3 * turn - 1, subs - 1)
        late = max(early, min(2 * turn + 2, subs - 1))
        events[early].append(functools.partial(push_early, far - turn))
        events[late].append(functools.partial(push_late, far - turn))
    waits = {point: [] for point in range(2 * subs)}
    for event in range(done, relays):
        turn = event // 2 - far + 1
        point = max(0, turn) if turn < 2 else 4 * turn - 4
        waits[point + event % 2 if turn > 0 else 0].append(functools.partial(relay, event))
    hops = subs - 1

    def arrive(distance):
        for flow in range(2):
            hop = (distance if flow == 1 else subs - distance) - 1
            for part in range(2):
                if hop == hops - 1:
                    gather(flow, hop, part).wait_recv()

    @pl.loop(0, subs)
    def _(place):
        distance = ring_distance(place, subs)
        target = sub_at(here + distance, subs)
        for spot in range(capacity):
            picked[spot] = table[index_ref[target, spot] + 1]
        for when in range(subs):
            if when == 0 or waits[2 * when]:

                @pl.when(place == when)
                def _():
                    if when == 0:
                        for away in range(1, subs):
                            side(away).wait()
                    for action in waits[2 * when]:
                        action()

        @pl.when(place == subs - 3)
        def _():
            arrive(1)
            arrive(subs - 1)

        wide_table[:count, :] = terms[distance]
        halves = aux_in[distance].astype(jnp.float32)
        info = jnp.concatenate([halves[:8, :], halves[8:, :]], axis=1)
        index = (info[feats : feats + 1, :] * 16.0 + info[feats + 1 : feats + 2, :]).astype(
            jnp.int32
        )
        chosen = pick(count, index)
        wide = jnp.concatenate(
            [chosen, jnp.concatenate([info, jnp.zeros_like(info)], axis=0).astype(jnp.bfloat16)],
            axis=0,
        )
        sent = jnp.concatenate([picked[:, part, :] for part in range(parts)], axis=1)
        summed = dot_t(wide, wide_table[...]) + sent
        message = norm(dot(silu(summed), square[3])).astype(jnp.bfloat16)
        acc[...] = dot(chosen, message)
        kept[place] = acc[...].astype(jnp.bfloat16)
        for when in range(subs):

            @pl.when(place == when)
            def _():
                for action in waits[2 * when + 1] + events[when]:
                    action()

    for part in range(pieces):
        span = slice(part * piece, (part + 1) * piece)
        total = acc[span, :]
        for flow in range(2):
            if has(flow, 1, part):
                pass_on(flow, 1, part).wait_recv()
                total = total + inbox[flow, 0, span, :].astype(jnp.float32)
        out_ref[span, :] = total.astype(jnp.bfloat16)
    for flow in range(2):
        for hop in range(hops):
            for part in range(2):
                gather(flow, hop, part).wait_send()
        for stage in range(1, far + 1):
            for part in range(pieces):
                if has(flow, stage, part):
                    pass_on(flow, stage, part).wait_send()


def partner(step, faces, subs):
    face, sub = lax.axis_index("face"), lax.axis_index("sub")
    return flip(face, lax.rem(step, faces), faces), flip(sub, step // faces, subs)


def flip(index, mask, count):
    total, bit = 0, 1
    while bit < count:
        total = total + lax.rem(lax.rem(index // bit, 2) + lax.rem(mask // bit, 2), 2) * bit
        bit *= 2
    return total


def processor_kernel(
    block,
    faces,
    subs,
    nodes_ref,
    sum_ref,
    halo_ref,
    source_ref,
    target_ref,
    edges_ref,
    feature_ref,
    *rest,
):
    weights, rest = rest[:9], rest[9:]
    (
        out_ref,
        held,
        held_sem,
        outgoing,
        arrived,
        local_table,
        base,
        acc,
        send_sem,
        recv_sem,
    ) = rest

    def fetch(place):
        return pltpu.make_async_copy(weights[place], held.at[place], held_sem.at[place])

    for place in range(len(weights)):
        fetch(place).start()

    def weight(place):
        fetch(place).wait()
        return held[place]

    devices = faces * subs
    me = lax.axis_index("face") * subs + lax.axis_index("sub")
    nodes, width = nodes_ref.shape
    slots = halo_ref.shape[1] // devices
    table_slots = devices * slots
    edges = source_ref.shape[1]
    barrier = pltpu.get_barrier_semaphore()

    @pl.loop(1, devices)
    def _(step):
        face, sub = partner(step, faces, subs)
        pl.semaphore_signal(barrier, inc=1, device_id=(face, sub), device_id_type=MESH_ID)

    start = nodes_ref[...]
    before = dot(start, weight(0)) + dot(sum_ref[...], weight(1))
    refined = norm(dot(silu(before), weight(2)))
    state = (start.astype(jnp.float32) + refined).astype(jnp.bfloat16)
    outgoing[...] = dot_t(pick(nodes, halo_ref[...]), state).astype(jnp.bfloat16)
    arrived[pl.ds(pl.multiple_of(me * slots, slots), slots), :] = jnp.zeros(
        (slots, width), jnp.bfloat16
    )
    pl.semaphore_wait(barrier, devices - 1)

    def copy(step):
        face, sub = partner(step, faces, subs)
        other = face * subs + sub
        return pltpu.make_async_remote_copy(
            src_ref=outgoing.at[pl.ds(pl.multiple_of(other * slots, slots), slots), :],
            dst_ref=arrived.at[pl.ds(pl.multiple_of(me * slots, slots), slots), :],
            send_sem=send_sem.at[step],
            recv_sem=recv_sem.at[step],
            device_id=(face, sub),
            device_id_type=MESH_ID,
        )

    @pl.loop(1, devices)
    def _(step):
        copy(devices - step).start()

    local_table[:nodes, :] = dot(state, weight(3)).astype(jnp.bfloat16)
    local_table[nodes : 2 * nodes, :] = dot(state, weight(4)).astype(jnp.bfloat16)
    local_table[2 * nodes :, :] = feature_ref[...]
    own_part = dot(state, weight(6))

    group = min(512, table_slots)
    source = source_ref[...]
    target = target_ref[...]
    tags = edges_ref[...]
    high = (target // 16).astype(jnp.float32)
    low = (target - (target // 16) * 16).astype(jnp.float32)
    digits = jnp.concatenate(
        [high, low, jnp.ones_like(high), jnp.zeros((13, edges), jnp.float32)], axis=0
    ).astype(jnp.bfloat16)
    info = jnp.concatenate([tags, digits], axis=0)
    spots = []
    for first in range(0, table_slots, group):
        rows = lax.broadcasted_iota(jnp.int32, (group, edges), 0) + (nodes + first)
        reads = jnp.where(rows == source, 1.0, 0.0).astype(jnp.bfloat16)
        found = lax.dot_general(
            reads, info, (((1,), (1,)), ((), ())), preferred_element_type=jnp.float32
        )
        spot = found[:, 16:17] * 16.0 + found[:, 17:18] + found[:, 18:19] - 1.0
        spot = spot.astype(jnp.int32)
        lanes = lax.broadcasted_iota(jnp.int32, (group, nodes), 1)
        chosen = jnp.where(lanes == spot, 1.0, 0.0).astype(jnp.bfloat16)
        base[first : first + group, :] = dot(chosen, local_table[nodes : 2 * nodes, :]) + dot(
            found[:, :16].astype(jnp.bfloat16), local_table[2 * nodes :, :]
        )
        spots.append(chosen)

    fetch(5).wait()
    for first in range(0, edges, block):
        span = slice(first, first + block)
        wide = jnp.concatenate(
            [
                pick(nodes, source_ref[:, span]),
                pick(nodes, target_ref[:, span]),
                edges_ref[:, span],
            ],
            axis=0,
        )
        total = dot_t(wide, local_table[...])
        message = norm(dot(silu(total), held[5])).astype(jnp.bfloat16)
        kept = jnp.where(source_ref[:, span] < nodes, target_ref[:, span], -1)
        if first == 0:
            acc[...] = dot(pick(nodes, kept), message)
        else:
            acc[...] += dot(pick(nodes, kept), message)

    @pl.loop(1, devices)
    def _(step):
        copy(devices - step).wait()

    for place, first in enumerate(range(0, table_slots, group)):
        span = slice(first, first + group)
        total = base[span, :] + dot(arrived[span, :], held[3])
        message = norm(dot(silu(total), held[5])).astype(jnp.bfloat16)
        acc[...] += dot_t(spots[place], message)
    after = own_part + dot(acc[...].astype(jnp.bfloat16), weight(7))
    final = norm(dot(silu(after), weight(8)))
    out_ref[...] = (state.astype(jnp.float32) + final).astype(jnp.bfloat16)


def vmem():
    return pl.BlockSpec(memory_space=pltpu.VMEM)


def smem():
    return pl.BlockSpec(memory_space=pltpu.SMEM)


def shards(
    grid_inputs,
    mesh_nodes,
    encoder_edges,
    mesh_edges,
    grid_send,
    node_receive,
    halo_send,
    edge_source,
    edge_target,
    embed_first,
    embed_second,
    encoder_feature,
    encoder_sender,
    encoder_receiver,
    encoder_output,
    updater_self,
    updater_message,
    updater_output,
    processor_feature,
    processor_sender,
    processor_receiver,
    processor_output,
    refiner_self,
    refiner_message,
    refiner_output,
):
    subs = lax.axis_size("sub")
    faces = lax.axis_size("face")
    devices = subs * faces
    grid_rows, inputs = grid_inputs.shape
    nodes, width = mesh_nodes.shape
    capacity = grid_send.shape[1]
    parts = width // LANES
    feats = encoder_edges.shape[0]

    anywhere = pl.BlockSpec(memory_space=pl.ANY)
    rows = min(512, grid_rows)
    pieces, far = 4, subs // 2
    summed = pl.pallas_call(
        functools.partial(encoder_kernel, rows, subs),
        out_shape=jax.ShapeDtypeStruct((nodes, width), jnp.bfloat16),
        in_specs=[smem(), vmem(), vmem(), vmem()] + [anywhere] * 7,
        out_specs=vmem(),
        scratch_shapes=[
            pltpu.VMEM((inputs, grid_rows), jnp.bfloat16),
            pltpu.VMEM((nodes, width), jnp.bfloat16),
            pltpu.VMEM((inputs, width), jnp.bfloat16),
            pltpu.VMEM((4, width, width), jnp.bfloat16),
            pltpu.SemaphoreType.DMA((6,)),
            pltpu.SemaphoreType.DMA((grid_rows // rows,)),
            pltpu.VMEM((grid_rows + 1, parts, LANES), jnp.float32),
            pltpu.VMEM((capacity, parts, LANES), jnp.float32),
            pltpu.VMEM((subs, 16, capacity // 2), jnp.bfloat16),
            pltpu.VMEM((subs, 16, capacity // 2), jnp.bfloat16),
            pltpu.VMEM((subs, nodes, width), jnp.bfloat16),
            pltpu.VMEM((nodes + 16, width), jnp.bfloat16),
            pltpu.VMEM((nodes, width), jnp.float32),
            pltpu.VMEM((subs, nodes, width), jnp.bfloat16),
            pltpu.VMEM((2, far, nodes, width), jnp.bfloat16),
            pltpu.VMEM((2, far, nodes, width), jnp.bfloat16),
            pltpu.SemaphoreType.DMA((subs,)),
            pltpu.SemaphoreType.DMA((subs,)),
            pltpu.SemaphoreType.DMA((2, 2 * (subs - 1))),
            pltpu.SemaphoreType.DMA((2, 2 * (subs - 1))),
            pltpu.SemaphoreType.DMA((2, far, pieces)),
            pltpu.SemaphoreType.DMA((2, far, pieces)),
        ],
        compiler_params=pltpu.CompilerParams(
            collective_id=1, has_side_effects=True, vmem_limit_bytes=60 * 2**20
        ),
        name="encoder",
    )(
        grid_send,
        encoder_edges,
        node_receive,
        encoder_feature,
        grid_inputs.T,
        mesh_nodes,
        embed_first,
        embed_second,
        encoder_sender,
        encoder_receiver,
        encoder_output,
    )

    pad_feature = lambda weight: jnp.pad(weight, ((0, 16 - feats), (0, 0)))
    edge_count = edge_source.shape[0]
    halo = halo_send.reshape(1, -1)
    step = min(512, edge_count)
    operands = (
        mesh_nodes,
        summed,
        halo,
        edge_source.reshape(1, -1),
        edge_target.reshape(1, -1),
        jnp.pad(mesh_edges, ((0, 16 - feats), (0, 0))),
        pad_feature(processor_feature),
        updater_self,
        updater_message,
        updater_output,
        processor_sender,
        processor_receiver,
        processor_output,
        refiner_self,
        refiner_message,
        refiner_output,
    )
    return pl.pallas_call(
        functools.partial(processor_kernel, step, faces, subs),
        out_shape=jax.ShapeDtypeStruct((nodes, width), jnp.bfloat16),
        in_specs=[vmem()] * (len(operands) - 9) + [anywhere] * 9,
        out_specs=vmem(),
        scratch_shapes=[
            pltpu.VMEM((9, width, width), jnp.bfloat16),
            pltpu.SemaphoreType.DMA((9,)),
            pltpu.VMEM((halo.shape[1], width), jnp.bfloat16),
            pltpu.VMEM((halo.shape[1], width), jnp.bfloat16),
            pltpu.VMEM((2 * nodes + 16, width), jnp.bfloat16),
            pltpu.VMEM((halo.shape[1], width), jnp.float32),
            pltpu.VMEM((nodes, width), jnp.float32),
            pltpu.SemaphoreType.DMA((devices,)),
            pltpu.SemaphoreType.DMA((devices,)),
        ],
        compiler_params=pltpu.CompilerParams(
            collective_id=0, has_side_effects=True, vmem_limit_bytes=60 * 2**20
        ),
        name="processor",
    )(*operands)


def solution(mesh):
    rows = P(("face", "sub"), None)
    placed = (
        rows,
        rows,
        P(None, ("face", "sub"), None),
        P(None, ("face", "sub")),
        rows,
        rows,
        rows,
        P(("face", "sub")),
        P(("face", "sub")),
    ) + (P(),) * 16
    return jax.shard_map(
        shards, mesh=mesh, in_specs=placed, out_specs=P(("face", "sub"), None), check_vma=False
    )
```

```python
import functools

import jax
import jax.numpy as jnp
from jax import lax
from jax.experimental import pallas as pl
from jax.experimental.pallas import tpu as pltpu
from jax.sharding import PartitionSpec as P

EPSILON = 1e-05
LANES = 128
MESH_ID = pl.DeviceIdType.MESH


def silu(values):
    half = values * 0.5
    return (half + half * jnp.tanh(half)).astype(jnp.bfloat16)


def norm(values):
    width = values.shape[-1]
    centered = values - jnp.sum(values, axis=-1, keepdims=True) * (1.0 / width)
    spread = jnp.sum(centered * centered, axis=-1, keepdims=True) * (1.0 / width)
    return centered * lax.rsqrt(spread + EPSILON)


def dot(a, b):
    return jnp.dot(a, b, preferred_element_type=jnp.float32)


def dot_t(a, b):
    return lax.dot_general(a, b, (((0,), (0,)), ((), ())), preferred_element_type=jnp.float32)


def pick(count, index):
    rows = lax.broadcasted_iota(jnp.int32, (count, index.shape[1]), 0)
    return jnp.where(rows == index, 1.0, 0.0).astype(jnp.bfloat16)


def sub_at(position, subs):
    position = lax.rem(position + subs, subs)
    return jnp.where(position < subs // 2, 2 * position, 2 * (subs - 1 - position) + 1)


def ring_position(subs):
    sub = lax.axis_index("sub")
    return jnp.where(lax.rem(sub, 2) == 0, sub // 2, subs - 1 - sub // 2)


def device_at(position, subs):
    return (lax.axis_index("face"), sub_at(position, subs))


def ring_distance(place, subs):
    half = lax.div(place + 1, 2)
    ahead = subs // 2 - half
    return jnp.where(lax.rem(place, 2) == 1, ahead, lax.rem(subs // 2 + half, subs))


def flip(index, mask, count):
    total, bit = 0, 1
    while bit < count:
        total = total + lax.rem(lax.rem(index // bit, 2) + lax.rem(mask // bit, 2), 2) * bit
        bit *= 2
    return total


def partner(step, faces, subs):
    face, sub = lax.axis_index("face"), lax.axis_index("sub")
    return flip(face, lax.rem(step, faces), faces), flip(sub, step // faces, subs)


def digits(values):
    high = lax.div(values + 16, 16) - 1
    low = values - high * 16
    return high.astype(jnp.float32), low.astype(jnp.float32)


def hot(index, count):
    lanes = lax.broadcasted_iota(jnp.int32, (index.shape[0], count), 1)
    return jnp.where(lanes == index, 1.0, 0.0).astype(jnp.bfloat16)


def dot_n(a, b):
    return lax.dot_general(a, b, (((1,), (1,)), ((), ())), preferred_element_type=jnp.float32)


def step_kernel(
    rows,
    block,
    faces,
    subs,
    index_ref,
    edges_ref,
    receive_ref,
    feature_ref,
    halo_ref,
    source_ref,
    target_ref,
    tags_ref,
    tag_feature_ref,
    x_hbm,
    nodes_hbm,
    first_hbm,
    second_hbm,
    sender_hbm,
    receiver_hbm,
    output_hbm,
    *rest,
):
    weights, rest = rest[:9], rest[9:]
    (
        out_ref,
        x,
        nodes,
        first,
        square,
        load_sem,
        x_sem,
        held,
        held_sem,
        table,
        picked,
        aux,
        aux_in,
        terms,
        wide_table,
        acc,
        kept,
        outbox,
        inbox,
        source,
        target,
        tags,
        before,
        leaving,
        spots,
        found,
        outgoing,
        arrived,
        base,
        local_table,
        side_send,
        side_recv,
        gather_send,
        gather_recv,
        sum_send,
        sum_recv,
        halo_send,
        halo_recv,
    ) = rest
    count, width = nodes.shape
    feats = edges_ref.shape[0]
    capacity = index_ref.shape[1]
    points = x.shape[1]
    parts = width // LANES
    far = subs // 2
    pieces = 4
    piece = count // pieces
    steps = points // rows
    here = ring_position(subs)
    barrier = pltpu.get_barrier_semaphore()

    @pl.loop(1, faces * subs)
    def _(step):
        pl.semaphore_signal(
            barrier, inc=1, device_id=partner(step, faces, subs), device_id_type=MESH_ID
        )

    devices = faces * subs
    me = lax.axis_index("face") * subs + lax.axis_index("sub")

    loads = [
        pltpu.make_async_copy(nodes_hbm, nodes, load_sem.at[0]),
        pltpu.make_async_copy(receiver_hbm, square.at[0], load_sem.at[1]),
        pltpu.make_async_copy(first_hbm, first, load_sem.at[2]),
        pltpu.make_async_copy(second_hbm, square.at[1], load_sem.at[3]),
        pltpu.make_async_copy(sender_hbm, square.at[2], load_sem.at[4]),
        pltpu.make_async_copy(output_hbm, square.at[3], load_sem.at[5]),
    ]

    def load_x(step):
        span = pl.ds(pl.multiple_of(step * rows, rows), rows)
        return pltpu.make_async_copy(x_hbm.at[:, span], x.at[:, span], x_sem.at[step])

    loads[0].start()
    loads[1].start()
    loads[2].start()
    load_x(0).start()
    loads[3].start()
    loads[4].start()

    @pl.loop(1, steps)
    def _(step):
        load_x(step).start()

    loads[5].start()

    def fetch(place):
        return pltpu.make_async_copy(weights[place], held.at[place], held_sem.at[place])

    def weight(place):
        fetch(place).wait()
        return held[place]

    for place in range(len(weights)):
        fetch(place).start()

    high, low = digits(receive_ref[...])
    features = [edges_ref[feat].astype(jnp.float32) for feat in range(feats)]
    fill = jnp.zeros((8 - feats - 2, capacity), jnp.float32)
    for sub in range(subs):
        span = slice(sub, sub + 1)
        stack = jnp.concatenate(
            [feature[span, :] for feature in features] + [high[span, :], low[span, :], fill], axis=0
        )
        aux[sub] = jnp.concatenate(
            [stack[:, : capacity // 2], stack[:, capacity // 2 :]], axis=0
        ).astype(jnp.bfloat16)
    table[0] = jnp.zeros((parts, LANES), jnp.float32)
    wide_table[count:, :] = jnp.zeros((16, width), jnp.bfloat16)
    wide_table[count : count + feats, :] = feature_ref[...]

    loads[0].wait()
    loads[1].wait()
    terms[0] = dot(nodes[...], square[0]).astype(jnp.bfloat16)
    pl.semaphore_wait(barrier, devices - 1)

    def gather(flow, hop, part):
        sign = 1 - 2 * flow
        span = pl.ds((2 * flow + part) * piece, piece)
        return pltpu.make_async_remote_copy(
            src_ref=terms.at[(-sign * hop) % subs, span, :],
            dst_ref=terms.at[(-sign * (hop + 1)) % subs, span, :],
            send_sem=gather_send.at[flow, 2 * hop + part],
            recv_sem=gather_recv.at[flow, 2 * hop + part],
            device_id=device_at(here + sign, subs),
            device_id_type=MESH_ID,
        )

    relays = 2 * (subs - 2)

    def relay(event):
        hop, part = event // 2 + 1, event % 2
        for flow in range(2):
            gather(flow, hop - 1, part).wait_recv()
            gather(flow, hop, part).start()

    def side(distance):
        return pltpu.make_async_remote_copy(
            src_ref=aux.at[sub_at(here + distance, subs)],
            dst_ref=aux_in.at[subs - distance],
            send_sem=side_send.at[distance],
            recv_sem=side_recv.at[distance],
            device_id=device_at(here + distance, subs),
            device_id_type=MESH_ID,
        )

    for part in range(2):
        for flow in range(2):
            gather(flow, 0, part).start()
    for distance in range(1, subs):
        side(distance).start()
    aux_in[0] = aux[sub_at(here, subs)]

    for load in loads[2:5]:
        load.wait()

    done = min(steps - 1, relays)

    @pl.loop(0, steps)
    def _(step):
        load_x(step).wait()
        start = pl.multiple_of(step * rows, rows)
        hidden = silu(dot_t(x[:, pl.ds(start, rows)], first[...]))
        latent = norm(dot(hidden, square[1])).astype(jnp.bfloat16)
        sent = dot(latent, square[2])
        for part in range(parts):
            table[pl.ds(start + 1, rows), part, :] = sent[:, part * LANES : (part + 1) * LANES]
        for event in range(done):

            @pl.when(step == event + 1)
            def _():
                relay(event)

    loads[5].wait()

    def pass_on(flow, stage, part):
        sign = 1 - 2 * flow
        span = pl.ds(part * piece, piece)
        return pltpu.make_async_remote_copy(
            src_ref=outbox.at[flow, stage - 1, span, :],
            dst_ref=inbox.at[flow, stage - 1, span, :],
            send_sem=sum_send.at[flow, stage - 1, part],
            recv_sem=sum_recv.at[flow, stage - 1, part],
            device_id=device_at(here + sign, subs),
            device_id_type=MESH_ID,
        )

    def has(flow, stage, part):
        return stage < far or part // 2 == flow

    def place_of(flow, stage):
        if stage == far:
            return 0
        return 2 * (far - stage) - 1 + flow

    def push(flow, stage, part):
        span = slice(part * piece, (part + 1) * piece)
        value = kept[place_of(flow, stage), span, :]
        if stage < far and has(flow, stage + 1, part):
            pass_on(flow, stage + 1, part).wait_recv()
            value = value.astype(jnp.float32) + inbox[flow, stage, span, :].astype(jnp.float32)
            value = value.astype(jnp.bfloat16)
        outbox[flow, stage - 1, span, :] = value
        pass_on(flow, stage, part).start()

    def push_early(stage):
        for part in range(2):
            for flow in range(2):
                if stage == far:
                    push(flow, stage, 2 * flow + part)
                else:
                    push(flow, stage, 2 * (1 - flow) + part)

    def push_late(stage):
        for part in range(2):
            for flow in range(2):
                push(flow, stage, 2 * flow + part)

    events = {place: [] for place in range(subs)}
    events[0].append(functools.partial(push_early, far))
    for turn in range(1, far - 1):
        early = min(3 * turn - 1, subs - 1)
        late = max(early, min(2 * turn + 2, subs - 1))
        events[early].append(functools.partial(push_early, far - turn))
        events[late].append(functools.partial(push_late, far - turn))
    waits = {point: [] for point in range(2 * subs)}
    for event in range(done, relays):
        turn = event // 2 - far + 1
        point = max(0, turn) if turn < 2 else 4 * turn - 4
        waits[point + event % 2 if turn > 0 else 0].append(functools.partial(relay, event))
    hops = subs - 1

    def arrive(distance):
        for flow in range(2):
            hop = (distance if flow == 1 else subs - distance) - 1
            for part in range(2):
                if hop == hops - 1:
                    gather(flow, hop, part).wait_recv()

    @pl.loop(0, subs)
    def _(place):
        distance = ring_distance(place, subs)
        sub = sub_at(here + distance, subs)
        for spot in range(capacity):
            picked[spot] = table[index_ref[sub, spot] + 1]
        for when in range(subs):
            if when == 0 or waits[2 * when]:

                @pl.when(place == when)
                def _():
                    if when == 0:
                        for away in range(1, subs):
                            side(away).wait()
                    for action in waits[2 * when]:
                        action()

        @pl.when(place == subs - 3)
        def _():
            arrive(1)
            arrive(subs - 1)

        wide_table[:count, :] = terms[distance]
        halves = aux_in[distance].astype(jnp.float32)
        info = jnp.concatenate([halves[:8, :], halves[8:, :]], axis=1)
        index = (info[feats : feats + 1, :] * 16.0 + info[feats + 1 : feats + 2, :]).astype(
            jnp.int32
        )
        chosen = pick(count, index)
        wide = jnp.concatenate(
            [chosen, jnp.concatenate([info, jnp.zeros_like(info)], axis=0).astype(jnp.bfloat16)],
            axis=0,
        )
        sent = jnp.concatenate([picked[:, part, :] for part in range(parts)], axis=1)
        summed = dot_t(wide, wide_table[...]) + sent
        message = norm(dot(silu(summed), square[3])).astype(jnp.bfloat16)
        acc[...] = dot(chosen, message)
        kept[place] = acc[...].astype(jnp.bfloat16)
        for when in range(subs):

            @pl.when(place == when)
            def _():
                for action in waits[2 * when + 1] + events[when]:
                    action()

    edges = target_ref.shape[0] * LANES
    slots, table_slots = halo_ref.shape[0], halo_ref.shape[0] * devices
    group = min(512, table_slots)
    for row in range(target_ref.shape[0]):
        span = slice(row * LANES, (row + 1) * LANES)
        source[:, span] = source_ref[row : row + 1, :]
        target[:, span] = target_ref[row : row + 1, :]
    tags[...] = jnp.zeros_like(tags)
    tags[:feats, :] = tags_ref[...]
    before[...] = dot(nodes[...], weight(0))
    high, low = digits(halo_ref[...])
    for start in range(0, table_slots, group):
        spot = lax.broadcasted_iota(jnp.int32, (group, devices), 0) + start
        peer = lax.broadcasted_iota(jnp.int32, (group, devices), 1)
        of_peer = jnp.where(lax.div(spot, slots) == peer, 1.0, 0.0).astype(jnp.bfloat16)
        lists = dot_n(of_peer, high.astype(jnp.bfloat16)) * 16.0
        lists = lists + dot_n(of_peer, low.astype(jnp.bfloat16))
        spot = lax.broadcasted_iota(jnp.int32, (group, slots), 0) + start
        place = lax.broadcasted_iota(jnp.int32, (group, slots), 1)
        index = jnp.sum(
            jnp.where(lax.rem(spot, slots) == place, lists, 0.0), axis=1, keepdims=True
        )
        leaving[start : start + group, :] = hot(index.astype(jnp.int32), count)
    arrived[pl.ds(pl.multiple_of(me * slots, slots), slots), :] = jnp.zeros(
        (slots, width), jnp.bfloat16
    )
    push_early(1)

    high, low = digits(target[...])
    info = jnp.concatenate(
        [
            tags[...],
            jnp.concatenate(
                [high, low, jnp.ones_like(high), jnp.zeros((13, edges), jnp.float32)], axis=0
            ).astype(jnp.bfloat16),
        ],
        axis=0,
    )
    for start in range(0, table_slots, group):
        span = slice(start, start + group)
        spot = lax.broadcasted_iota(jnp.int32, (group, edges), 0) + (count + start)
        reads = jnp.where(spot == source[...], 1.0, 0.0).astype(jnp.bfloat16)
        read = dot_n(reads, info)
        index = read[:, 16:17] * 16.0 + read[:, 17:18] + read[:, 18:19] - 1.0
        chosen = hot(index.astype(jnp.int32), count)
        found[span, :] = jnp.concatenate([chosen, read[:, :16].astype(jnp.bfloat16)], axis=1)
        spots[:, span] = chosen.T
    push_late(1)
    local_table[2 * count :, :] = jnp.zeros((16, width), jnp.bfloat16)
    local_table[2 * count : 2 * count + feats, :] = tag_feature_ref[...]

    totals = []
    for part in range(pieces):
        span = slice(part * piece, (part + 1) * piece)
        total = acc[span, :]
        for flow in range(2):
            if has(flow, 1, part):
                pass_on(flow, 1, part).wait_recv()
                total = total + inbox[flow, 0, span, :].astype(jnp.float32)
        totals.append(total.astype(jnp.bfloat16))
    total = before[...] + dot(jnp.concatenate(totals, axis=0), weight(1))
    refined = norm(dot(silu(total), weight(2)))
    state = (nodes[...].astype(jnp.float32) + refined).astype(jnp.bfloat16)
    for start in range(0, table_slots, group):
        span = slice(start, start + group)
        outgoing[span, :] = dot(leaving[span, :], state).astype(jnp.bfloat16)

    def copy(step):
        face, sub = partner(step, faces, subs)
        other = face * subs + sub
        return pltpu.make_async_remote_copy(
            src_ref=outgoing.at[pl.ds(pl.multiple_of(other * slots, slots), slots), :],
            dst_ref=arrived.at[pl.ds(pl.multiple_of(me * slots, slots), slots), :],
            send_sem=halo_send.at[step],
            recv_sem=halo_recv.at[step],
            device_id=(face, sub),
            device_id_type=MESH_ID,
        )

    @pl.loop(1, devices)
    def _(step):
        copy(devices - step).start()

    local_table[:count, :] = dot(state, weight(3)).astype(jnp.bfloat16)
    local_table[count : 2 * count, :] = dot(state, weight(4)).astype(jnp.bfloat16)
    own_part = dot(state, weight(6))
    for start in range(0, table_slots, group):
        span = slice(start, start + group)
        base[span, :] = dot(found[span, :], local_table[count:, :])
    fetch(5).wait()
    for start in range(0, edges, block):
        span = slice(start, start + block)
        senders, receivers = source[:, span], target[:, span]
        wide = jnp.concatenate(
            [pick(count, senders), pick(count, receivers), tags[:, span]], axis=0
        )
        message = norm(dot(silu(dot_t(wide, local_table[...])), held[5])).astype(jnp.bfloat16)
        chosen = pick(count, jnp.where(senders < count, receivers, -1))
        if start == 0:
            acc[...] = dot(chosen, message)
        else:
            acc[...] += dot(chosen, message)
    for flow in range(2):
        for hop in range(hops):
            for part in range(2):
                gather(flow, hop, part).wait_send()
        for stage in range(1, far + 1):
            for part in range(pieces):
                if has(flow, stage, part):
                    pass_on(flow, stage, part).wait_send()
    fetch(7).wait()
    fetch(8).wait()

    @pl.loop(1, devices)
    def _(step):
        copy(devices - step).wait()

    for start in range(0, table_slots, group):
        span = slice(start, start + group)
        total = base[span, :] + dot(arrived[span, :], held[3])
        message = norm(dot(silu(total), held[5])).astype(jnp.bfloat16)
        acc[...] += dot(spots[:, span], message)
    after = own_part + dot(acc[...].astype(jnp.bfloat16), held[7])
    final = norm(dot(silu(after), held[8]))
    out_ref[...] = (state.astype(jnp.float32) + final).astype(jnp.bfloat16)


def vmem():
    return pl.BlockSpec(memory_space=pltpu.VMEM)


def smem():
    return pl.BlockSpec(memory_space=pltpu.SMEM)


def shards(
    grid_inputs,
    mesh_nodes,
    encoder_edges,
    mesh_edges,
    grid_send,
    node_receive,
    halo_send,
    edge_source,
    edge_target,
    embed_first,
    embed_second,
    encoder_feature,
    encoder_sender,
    encoder_receiver,
    encoder_output,
    updater_self,
    updater_message,
    updater_output,
    processor_feature,
    processor_sender,
    processor_receiver,
    processor_output,
    refiner_self,
    refiner_message,
    refiner_output,
):
    subs = lax.axis_size("sub")
    faces = lax.axis_size("face")
    devices = subs * faces
    grid_rows, inputs = grid_inputs.shape
    nodes, width = mesh_nodes.shape
    capacity = grid_send.shape[1]
    parts = width // LANES
    feats = encoder_edges.shape[0]

    anywhere = pl.BlockSpec(memory_space=pl.ANY)
    rows = min(512, grid_rows)
    pieces, far = 4, subs // 2
    edge_count = edge_source.shape[0]
    table_slots = devices * halo_send.shape[1]
    bf16, f32 = jnp.bfloat16, jnp.float32
    return pl.pallas_call(
        functools.partial(step_kernel, rows, min(512, edge_count), faces, subs),
        out_shape=jax.ShapeDtypeStruct((nodes, width), bf16),
        in_specs=[smem()] + [vmem()] * 8 + [anywhere] * 16,
        out_specs=vmem(),
        scratch_shapes=[
            pltpu.VMEM((inputs, grid_rows), bf16),
            pltpu.VMEM((nodes, width), bf16),
            pltpu.VMEM((inputs, width), bf16),
            pltpu.VMEM((4, width, width), bf16),
            pltpu.SemaphoreType.DMA((6,)),
            pltpu.SemaphoreType.DMA((grid_rows // rows,)),
            pltpu.VMEM((9, width, width), bf16),
            pltpu.SemaphoreType.DMA((9,)),
            pltpu.VMEM((grid_rows + 1, parts, LANES), f32),
            pltpu.VMEM((capacity, parts, LANES), f32),
            pltpu.VMEM((subs, 16, capacity // 2), bf16),
            pltpu.VMEM((subs, 16, capacity // 2), bf16),
            pltpu.VMEM((subs, nodes, width), bf16),
            pltpu.VMEM((nodes + 16, width), bf16),
            pltpu.VMEM((nodes, width), f32),
            pltpu.VMEM((subs, nodes, width), bf16),
            pltpu.VMEM((2, far, nodes, width), bf16),
            pltpu.VMEM((2, far, nodes, width), bf16),
            pltpu.VMEM((1, edge_count), jnp.int32),
            pltpu.VMEM((1, edge_count), jnp.int32),
            pltpu.VMEM((16, edge_count), bf16),
            pltpu.VMEM((nodes, width), f32),
            pltpu.VMEM((table_slots, nodes), bf16),
            pltpu.VMEM((nodes, table_slots), bf16),
            pltpu.VMEM((table_slots, nodes + 16), bf16),
            pltpu.VMEM((table_slots, width), bf16),
            pltpu.VMEM((table_slots, width), bf16),
            pltpu.VMEM((table_slots, width), f32),
            pltpu.VMEM((2 * nodes + 16, width), bf16),
            pltpu.SemaphoreType.DMA((subs,)),
            pltpu.SemaphoreType.DMA((subs,)),
            pltpu.SemaphoreType.DMA((2, 2 * (subs - 1))),
            pltpu.SemaphoreType.DMA((2, 2 * (subs - 1))),
            pltpu.SemaphoreType.DMA((2, far, pieces)),
            pltpu.SemaphoreType.DMA((2, far, pieces)),
            pltpu.SemaphoreType.DMA((devices,)),
            pltpu.SemaphoreType.DMA((devices,)),
        ],
        compiler_params=pltpu.CompilerParams(
            collective_id=1, has_side_effects=True, vmem_limit_bytes=63 * 2**20
        ),
        name="step",
    )(
        grid_send,
        encoder_edges,
        node_receive,
        encoder_feature,
        halo_send.T,
        edge_source.reshape(-1, LANES),
        edge_target.reshape(-1, LANES),
        mesh_edges,
        processor_feature,
        grid_inputs.T,
        mesh_nodes,
        embed_first,
        embed_second,
        encoder_sender,
        encoder_receiver,
        encoder_output,
        updater_self,
        updater_message,
        updater_output,
        processor_sender,
        processor_receiver,
        processor_output,
        refiner_self,
        refiner_message,
        refiner_output,
    )


def solution(mesh):
    rows = P(("face", "sub"), None)
    placed = (
        rows,
        rows,
        P(None, ("face", "sub"), None),
        P(None, ("face", "sub")),
        rows,
        rows,
        rows,
        P(("face", "sub")),
        P(("face", "sub")),
    ) + (P(),) * 16
    return jax.shard_map(
        shards, mesh=mesh, in_specs=placed, out_specs=P(("face", "sub"), None), check_vma=False
    )
```

```python
import functools

import jax
import jax.numpy as jnp
from jax import lax
from jax.experimental import pallas as pl
from jax.experimental.pallas import tpu as pltpu
from jax.sharding import PartitionSpec as P

EPSILON = 1e-05
LANES = 128
MESH_ID = pl.DeviceIdType.MESH


def silu(values):
    half = values * 0.5
    return (half + half * jnp.tanh(half)).astype(jnp.bfloat16)


def norm(values):
    width = values.shape[-1]
    centered = values - jnp.sum(values, axis=-1, keepdims=True) * (1.0 / width)
    spread = jnp.sum(centered * centered, axis=-1, keepdims=True) * (1.0 / width)
    return centered * lax.rsqrt(spread + EPSILON)


def dot(a, b):
    return jnp.dot(a, b, preferred_element_type=jnp.float32)


def dot_t(a, b):
    return lax.dot_general(a, b, (((0,), (0,)), ((), ())), preferred_element_type=jnp.float32)


def pick(count, index):
    rows = lax.broadcasted_iota(jnp.int32, (count, index.shape[1]), 0)
    return jnp.where(rows == index, 1.0, 0.0).astype(jnp.bfloat16)


def sub_at(position, subs):
    position = lax.rem(position + subs, subs)
    return jnp.where(position < subs // 2, 2 * position, 2 * (subs - 1 - position) + 1)


def ring_position(subs):
    sub = lax.axis_index("sub")
    return jnp.where(lax.rem(sub, 2) == 0, sub // 2, subs - 1 - sub // 2)


def device_at(position, subs):
    return (lax.axis_index("face"), sub_at(position, subs))


def ring_distance(place, subs):
    half = lax.div(place + 1, 2)
    ahead = subs // 2 - half
    return jnp.where(lax.rem(place, 2) == 1, ahead, lax.rem(subs // 2 + half, subs))


def flips(index, count):
    bits = [(bit, lax.rem(lax.div(index, 1 << bit), 2)) for bit in range((count - 1).bit_length())]
    return [
        sum((((1 - value) if mask >> bit & 1 else value) << bit for bit, value in bits), 0)
        for mask in range(count)
    ]


def partners(faces, subs):
    face = flips(lax.axis_index("face"), faces)
    sub = flips(lax.axis_index("sub"), subs)
    return [(face[step % faces], sub[step // faces]) for step in range(faces * subs - 1, 0, -1)]


def digits(values):
    high = lax.div(values + 16, 16) - 1
    low = values - high * 16
    return high.astype(jnp.float32), low.astype(jnp.float32)


def hot(index, count):
    lanes = lax.broadcasted_iota(jnp.int32, (index.shape[0], count), 1)
    return jnp.where(lanes == index, 1.0, 0.0).astype(jnp.bfloat16)


def dot_n(a, b):
    return lax.dot_general(a, b, (((1,), (1,)), ((), ())), preferred_element_type=jnp.float32)


def step_kernel(
    rows,
    block,
    faces,
    subs,
    index_ref,
    edges_ref,
    receive_ref,
    feature_ref,
    halo_ref,
    source_ref,
    target_ref,
    tags_ref,
    tag_feature_ref,
    x_hbm,
    nodes_hbm,
    first_hbm,
    second_hbm,
    sender_hbm,
    receiver_hbm,
    output_hbm,
    *rest,
):
    weights, rest = rest[:9], rest[9:]
    (
        out_ref,
        x,
        nodes,
        first,
        square,
        load_sem,
        x_sem,
        held,
        held_sem,
        table,
        picked,
        aux,
        aux_in,
        terms,
        wide_table,
        acc,
        kept,
        outbox,
        inbox,
        source,
        target,
        tags,
        before,
        leaving,
        spots,
        found,
        outgoing,
        arrived,
        base,
        local_table,
        side_send,
        side_recv,
        gather_send,
        gather_recv,
        sum_send,
        sum_recv,
        halo_send,
        halo_recv,
    ) = rest
    count, width = nodes.shape
    feats = edges_ref.shape[0]
    capacity = index_ref.shape[1]
    points = x.shape[1]
    parts = width // LANES
    far = subs // 2
    pieces = 4
    piece = count // pieces
    steps = points // rows
    here = ring_position(subs)
    barrier = pltpu.get_barrier_semaphore()

    others = partners(faces, subs)
    for other in others:
        pl.semaphore_signal(barrier, inc=1, device_id=other, device_id_type=MESH_ID)

    devices = faces * subs
    me = lax.axis_index("face") * subs + lax.axis_index("sub")

    loads = [
        pltpu.make_async_copy(nodes_hbm, nodes, load_sem.at[0]),
        pltpu.make_async_copy(receiver_hbm, square.at[0], load_sem.at[1]),
        pltpu.make_async_copy(first_hbm, first, load_sem.at[2]),
        pltpu.make_async_copy(second_hbm, square.at[1], load_sem.at[3]),
        pltpu.make_async_copy(sender_hbm, square.at[2], load_sem.at[4]),
        pltpu.make_async_copy(output_hbm, square.at[3], load_sem.at[5]),
    ]

    def load_x(step):
        span = pl.ds(pl.multiple_of(step * rows, rows), rows)
        return pltpu.make_async_copy(x_hbm.at[:, span], x.at[:, span], x_sem.at[step])

    loads[0].start()
    loads[1].start()
    loads[2].start()
    load_x(0).start()
    loads[3].start()
    loads[4].start()

    @pl.loop(1, steps)
    def _(step):
        load_x(step).start()

    loads[5].start()

    def fetch(place):
        return pltpu.make_async_copy(weights[place], held.at[place], held_sem.at[place])

    def weight(place):
        fetch(place).wait()
        return held[place]

    for place in range(len(weights)):
        fetch(place).start()

    loads[0].wait()
    loads[1].wait()
    terms[0] = dot(nodes[...], square[0]).astype(jnp.bfloat16)
    pl.semaphore_wait(barrier, devices - 1)

    def gather(flow, hop, part):
        sign = 1 - 2 * flow
        span = pl.ds((2 * flow + part) * piece, piece)
        return pltpu.make_async_remote_copy(
            src_ref=terms.at[(-sign * hop) % subs, span, :],
            dst_ref=terms.at[(-sign * (hop + 1)) % subs, span, :],
            send_sem=gather_send.at[flow, 2 * hop + part],
            recv_sem=gather_recv.at[flow, 2 * hop + part],
            device_id=device_at(here + sign, subs),
            device_id_type=MESH_ID,
        )

    relays = 2 * (subs - 2)

    def relay(event):
        hop, part = event // 2 + 1, event % 2
        for flow in range(2):
            gather(flow, hop - 1, part).wait_recv()
            gather(flow, hop, part).start()

    def side(distance):
        return pltpu.make_async_remote_copy(
            src_ref=aux.at[sub_at(here + distance, subs)],
            dst_ref=aux_in.at[subs - distance],
            send_sem=side_send.at[distance],
            recv_sem=side_recv.at[distance],
            device_id=device_at(here + distance, subs),
            device_id_type=MESH_ID,
        )

    for part in range(2):
        for flow in range(2):
            gather(flow, 0, part).start()
    high, low = digits(receive_ref[...])
    features = [edges_ref[feat].astype(jnp.float32) for feat in range(feats)]
    fill = jnp.zeros((8 - feats - 2, capacity), jnp.float32)
    for sub in range(subs):
        span = slice(sub, sub + 1)
        stack = jnp.concatenate(
            [feature[span, :] for feature in features] + [high[span, :], low[span, :], fill], axis=0
        )
        aux[sub] = jnp.concatenate(
            [stack[:, : capacity // 2], stack[:, capacity // 2 :]], axis=0
        ).astype(jnp.bfloat16)
    table[0] = jnp.zeros((parts, LANES), jnp.float32)
    wide_table[count:, :] = jnp.zeros((16, width), jnp.bfloat16)
    wide_table[count : count + feats, :] = feature_ref[...]

    for distance in range(1, subs):
        side(distance).start()
    aux_in[0] = aux[sub_at(here, subs)]

    for load in loads[2:5]:
        load.wait()

    done = min(steps - 1, relays)

    @pl.loop(0, steps)
    def _(step):
        load_x(step).wait()
        start = pl.multiple_of(step * rows, rows)
        hidden = silu(dot_t(x[:, pl.ds(start, rows)], first[...]))
        latent = norm(dot(hidden, square[1])).astype(jnp.bfloat16)
        sent = dot(latent, square[2])
        for part in range(parts):
            table[pl.ds(start + 1, rows), part, :] = sent[:, part * LANES : (part + 1) * LANES]
        for event in range(done):

            @pl.when(step == event + 1)
            def _():
                relay(event)

    loads[5].wait()

    def pass_on(flow, stage, part):
        sign = 1 - 2 * flow
        span = pl.ds(part * piece, piece)
        return pltpu.make_async_remote_copy(
            src_ref=outbox.at[flow, stage - 1, span, :],
            dst_ref=inbox.at[flow, stage - 1, span, :],
            send_sem=sum_send.at[flow, stage - 1, part],
            recv_sem=sum_recv.at[flow, stage - 1, part],
            device_id=device_at(here + sign, subs),
            device_id_type=MESH_ID,
        )

    def has(flow, stage, part):
        return stage < far or part // 2 == flow

    def place_of(flow, stage):
        if stage == far:
            return 0
        return 2 * (far - stage) - 1 + flow

    def push(flow, stage, part):
        span = slice(part * piece, (part + 1) * piece)
        value = kept[place_of(flow, stage), span, :]
        if stage < far and has(flow, stage + 1, part):
            pass_on(flow, stage + 1, part).wait_recv()
            value = value.astype(jnp.float32) + inbox[flow, stage, span, :].astype(jnp.float32)
            value = value.astype(jnp.bfloat16)
        outbox[flow, stage - 1, span, :] = value
        pass_on(flow, stage, part).start()

    def push_early(stage):
        for part in range(2):
            for flow in range(2):
                if stage == far:
                    push(flow, stage, 2 * flow + part)
                else:
                    push(flow, stage, 2 * (1 - flow) + part)

    def push_late(stage):
        for part in range(2):
            for flow in range(2):
                push(flow, stage, 2 * flow + part)

    events = {place: [] for place in range(subs)}
    events[0].append(functools.partial(push_early, far))
    for turn in range(1, far - 1):
        early = min(3 * turn - 1, subs - 1)
        late = max(early, min(2 * turn + 2, subs - 1))
        events[early].append(functools.partial(push_early, far - turn))
        events[late].append(functools.partial(push_late, far - turn))
    waits = {point: [] for point in range(2 * subs)}
    for event in range(done, relays):
        turn = event // 2 - far + 1
        point = max(0, turn) if turn < 2 else 4 * turn - 4
        waits[point + event % 2 if turn > 0 else 0].append(functools.partial(relay, event))
    hops = subs - 1

    def arrive(distance):
        for flow in range(2):
            hop = (distance if flow == 1 else subs - distance) - 1
            for part in range(2):
                if hop == hops - 1:
                    gather(flow, hop, part).wait_recv()

    @pl.loop(0, subs)
    def _(place):
        distance = ring_distance(place, subs)
        sub = sub_at(here + distance, subs)
        for spot in range(capacity):
            picked[spot] = table[index_ref[sub, spot] + 1]
        for when in range(subs):
            if when == 0 or waits[2 * when]:

                @pl.when(place == when)
                def _():
                    if when == 0:
                        for away in range(1, subs):
                            side(away).wait()
                    for action in waits[2 * when]:
                        action()

        @pl.when(place == subs - 3)
        def _():
            arrive(1)
            arrive(subs - 1)

        wide_table[:count, :] = terms[distance]
        halves = aux_in[distance].astype(jnp.float32)
        info = jnp.concatenate([halves[:8, :], halves[8:, :]], axis=1)
        index = (info[feats : feats + 1, :] * 16.0 + info[feats + 1 : feats + 2, :]).astype(
            jnp.int32
        )
        chosen = pick(count, index)
        wide = jnp.concatenate(
            [chosen, jnp.concatenate([info, jnp.zeros_like(info)], axis=0).astype(jnp.bfloat16)],
            axis=0,
        )
        sent = jnp.concatenate([picked[:, part, :] for part in range(parts)], axis=1)
        summed = dot_t(wide, wide_table[...]) + sent
        message = norm(dot(silu(summed), square[3])).astype(jnp.bfloat16)
        acc[...] = dot(chosen, message)
        kept[place] = acc[...].astype(jnp.bfloat16)
        for when in range(subs):

            @pl.when(place == when)
            def _():
                for action in waits[2 * when + 1] + events[when]:
                    action()

    push_early(1)
    push_late(1)

    edges = target_ref.shape[0] * LANES
    slots, table_slots = halo_ref.shape[0], halo_ref.shape[0] * devices
    group = min(512, table_slots)
    for row in range(target_ref.shape[0]):
        span = slice(row * LANES, (row + 1) * LANES)
        source[:, span] = source_ref[row : row + 1, :]
        target[:, span] = target_ref[row : row + 1, :]
    tags[...] = jnp.zeros_like(tags)
    tags[:feats, :] = tags_ref[...]
    before[...] = dot(nodes[...], weight(0))
    high, low = digits(halo_ref[...])
    for start in range(0, table_slots, group):
        spot = lax.broadcasted_iota(jnp.int32, (group, devices), 0) + start
        peer = lax.broadcasted_iota(jnp.int32, (group, devices), 1)
        of_peer = jnp.where(lax.div(spot, slots) == peer, 1.0, 0.0).astype(jnp.bfloat16)
        lists = dot_n(of_peer, high.astype(jnp.bfloat16)) * 16.0
        lists = lists + dot_n(of_peer, low.astype(jnp.bfloat16))
        spot = lax.broadcasted_iota(jnp.int32, (group, slots), 0) + start
        place = lax.broadcasted_iota(jnp.int32, (group, slots), 1)
        index = jnp.sum(
            jnp.where(lax.rem(spot, slots) == place, lists, 0.0), axis=1, keepdims=True
        )
        leaving[start : start + group, :] = hot(index.astype(jnp.int32), count)
    arrived[pl.ds(pl.multiple_of(me * slots, slots), slots), :] = jnp.zeros(
        (slots, width), jnp.bfloat16
    )
    high, low = digits(target[...])
    info = jnp.concatenate(
        [
            tags[...],
            jnp.concatenate(
                [high, low, jnp.ones_like(high), jnp.zeros((13, edges), jnp.float32)], axis=0
            ).astype(jnp.bfloat16),
        ],
        axis=0,
    )
    for start in range(0, table_slots, group):
        span = slice(start, start + group)
        spot = lax.broadcasted_iota(jnp.int32, (group, edges), 0) + (count + start)
        reads = jnp.where(spot == source[...], 1.0, 0.0).astype(jnp.bfloat16)
        read = dot_n(reads, info)
        index = read[:, 16:17] * 16.0 + read[:, 17:18] + read[:, 18:19] - 1.0
        chosen = hot(index.astype(jnp.int32), count)
        found[span, :] = jnp.concatenate([chosen, read[:, :16].astype(jnp.bfloat16)], axis=1)
        spots[:, span] = chosen.T
    local_table[2 * count :, :] = jnp.zeros((16, width), jnp.bfloat16)
    local_table[2 * count : 2 * count + feats, :] = tag_feature_ref[...]

    totals = []
    for part in range(pieces):
        span = slice(part * piece, (part + 1) * piece)
        total = acc[span, :]
        for flow in range(2):
            if has(flow, 1, part):
                pass_on(flow, 1, part).wait_recv()
                total = total + inbox[flow, 0, span, :].astype(jnp.float32)
        totals.append(total.astype(jnp.bfloat16))
    total = before[...] + dot(jnp.concatenate(totals, axis=0), weight(1))
    refined = norm(dot(silu(total), weight(2)))
    state = (nodes[...].astype(jnp.float32) + refined).astype(jnp.bfloat16)
    for start in range(0, table_slots, group):
        span = slice(start, start + group)
        outgoing[span, :] = dot(leaving[span, :], state).astype(jnp.bfloat16)

    def copy(step):
        face, sub = others[step]
        other = face * subs + sub
        return pltpu.make_async_remote_copy(
            src_ref=outgoing.at[pl.ds(pl.multiple_of(other * slots, slots), slots), :],
            dst_ref=arrived.at[pl.ds(pl.multiple_of(me * slots, slots), slots), :],
            send_sem=halo_send.at[step],
            recv_sem=halo_recv.at[step],
            device_id=(face, sub),
            device_id_type=MESH_ID,
        )

    for step in range(devices - 1):
        copy(step).start()

    local_table[:count, :] = dot(state, weight(3)).astype(jnp.bfloat16)
    local_table[count : 2 * count, :] = dot(state, weight(4)).astype(jnp.bfloat16)
    own_part = dot(state, weight(6))
    for start in range(0, table_slots, group):
        span = slice(start, start + group)
        base[span, :] = dot(found[span, :], local_table[count:, :])
    fetch(5).wait()
    for start in range(0, edges, block):
        span = slice(start, start + block)
        senders, receivers = source[:, span], target[:, span]
        wide = jnp.concatenate(
            [pick(count, senders), pick(count, receivers), tags[:, span]], axis=0
        )
        message = norm(dot(silu(dot_t(wide, local_table[...])), held[5])).astype(jnp.bfloat16)
        chosen = pick(count, jnp.where(senders < count, receivers, -1))
        if start == 0:
            acc[...] = dot(chosen, message)
        else:
            acc[...] += dot(chosen, message)
    for flow in range(2):
        for hop in range(hops):
            for part in range(2):
                gather(flow, hop, part).wait_send()
        for stage in range(1, far + 1):
            for part in range(pieces):
                if has(flow, stage, part):
                    pass_on(flow, stage, part).wait_send()
    fetch(7).wait()
    fetch(8).wait()

    for step in range(devices - 1):
        copy(step).wait()

    for start in range(0, table_slots, group):
        span = slice(start, start + group)
        total = base[span, :] + dot(arrived[span, :], held[3])
        message = norm(dot(silu(total), held[5])).astype(jnp.bfloat16)
        acc[...] += dot(spots[:, span], message)
    after = own_part + dot(acc[...].astype(jnp.bfloat16), held[7])
    final = norm(dot(silu(after), held[8]))
    out_ref[...] = (state.astype(jnp.float32) + final).astype(jnp.bfloat16)


def vmem():
    return pl.BlockSpec(memory_space=pltpu.VMEM)


def smem():
    return pl.BlockSpec(memory_space=pltpu.SMEM)


def shards(
    grid_inputs,
    mesh_nodes,
    encoder_edges,
    mesh_edges,
    grid_send,
    node_receive,
    halo_send,
    edge_source,
    edge_target,
    embed_first,
    embed_second,
    encoder_feature,
    encoder_sender,
    encoder_receiver,
    encoder_output,
    updater_self,
    updater_message,
    updater_output,
    processor_feature,
    processor_sender,
    processor_receiver,
    processor_output,
    refiner_self,
    refiner_message,
    refiner_output,
):
    subs = lax.axis_size("sub")
    faces = lax.axis_size("face")
    devices = subs * faces
    grid_rows, inputs = grid_inputs.shape
    nodes, width = mesh_nodes.shape
    capacity = grid_send.shape[1]
    parts = width // LANES
    feats = encoder_edges.shape[0]

    anywhere = pl.BlockSpec(memory_space=pl.ANY)
    rows = min(512, grid_rows)
    pieces, far = 4, subs // 2
    edge_count = edge_source.shape[0]
    table_slots = devices * halo_send.shape[1]
    bf16, f32 = jnp.bfloat16, jnp.float32
    return pl.pallas_call(
        functools.partial(step_kernel, rows, min(512, edge_count), faces, subs),
        out_shape=jax.ShapeDtypeStruct((nodes, width), bf16),
        in_specs=[smem()] + [vmem()] * 8 + [anywhere] * 16,
        out_specs=vmem(),
        scratch_shapes=[
            pltpu.VMEM((inputs, grid_rows), bf16),
            pltpu.VMEM((nodes, width), bf16),
            pltpu.VMEM((inputs, width), bf16),
            pltpu.VMEM((4, width, width), bf16),
            pltpu.SemaphoreType.DMA((6,)),
            pltpu.SemaphoreType.DMA((grid_rows // rows,)),
            pltpu.VMEM((9, width, width), bf16),
            pltpu.SemaphoreType.DMA((9,)),
            pltpu.VMEM((grid_rows + 1, parts, LANES), f32),
            pltpu.VMEM((capacity, parts, LANES), f32),
            pltpu.VMEM((subs, 16, capacity // 2), bf16),
            pltpu.VMEM((subs, 16, capacity // 2), bf16),
            pltpu.VMEM((subs, nodes, width), bf16),
            pltpu.VMEM((nodes + 16, width), bf16),
            pltpu.VMEM((nodes, width), f32),
            pltpu.VMEM((subs, nodes, width), bf16),
            pltpu.VMEM((2, far, nodes, width), bf16),
            pltpu.VMEM((2, far, nodes, width), bf16),
            pltpu.VMEM((1, edge_count), jnp.int32),
            pltpu.VMEM((1, edge_count), jnp.int32),
            pltpu.VMEM((16, edge_count), bf16),
            pltpu.VMEM((nodes, width), f32),
            pltpu.VMEM((table_slots, nodes), bf16),
            pltpu.VMEM((nodes, table_slots), bf16),
            pltpu.VMEM((table_slots, nodes + 16), bf16),
            pltpu.VMEM((table_slots, width), bf16),
            pltpu.VMEM((table_slots, width), bf16),
            pltpu.VMEM((table_slots, width), f32),
            pltpu.VMEM((2 * nodes + 16, width), bf16),
            pltpu.SemaphoreType.DMA((subs,)),
            pltpu.SemaphoreType.DMA((subs,)),
            pltpu.SemaphoreType.DMA((2, 2 * (subs - 1))),
            pltpu.SemaphoreType.DMA((2, 2 * (subs - 1))),
            pltpu.SemaphoreType.DMA((2, far, pieces)),
            pltpu.SemaphoreType.DMA((2, far, pieces)),
            pltpu.SemaphoreType.DMA((devices,)),
            pltpu.SemaphoreType.DMA((devices,)),
        ],
        compiler_params=pltpu.CompilerParams(
            collective_id=1, has_side_effects=True, vmem_limit_bytes=63 * 2**20
        ),
        name="step",
    )(
        grid_send,
        encoder_edges,
        node_receive,
        encoder_feature,
        halo_send.T,
        edge_source.reshape(-1, LANES),
        edge_target.reshape(-1, LANES),
        mesh_edges,
        processor_feature,
        grid_inputs.T,
        mesh_nodes,
        embed_first,
        embed_second,
        encoder_sender,
        encoder_receiver,
        encoder_output,
        updater_self,
        updater_message,
        updater_output,
        processor_sender,
        processor_receiver,
        processor_output,
        refiner_self,
        refiner_message,
        refiner_output,
    )


def solution(mesh):
    rows = P(("face", "sub"), None)
    placed = (
        rows,
        rows,
        P(None, ("face", "sub"), None),
        P(None, ("face", "sub")),
        rows,
        rows,
        rows,
        P(("face", "sub")),
        P(("face", "sub")),
    ) + (P(),) * 16
    return jax.shard_map(
        shards, mesh=mesh, in_specs=placed, out_specs=P(("face", "sub"), None), check_vma=False
    )
```
